256 devices in a mesh: rows: 32 (over z_hi, y, core), cols: 8 (over x, z_lo).
Axes of the slice: x: 4, y: 4, z: 8 (z_hi: 4, z_lo: 2; z = z_hi * 2 + z_lo), core: 2. Of those that a mesh axis runs over, the one named last changes fastest.
Arguments:
- pair: bfloat16 [768, 768, 128], P('rows', 'cols'), may hold values from -6 to 6
- token_mask: int32 [768], P('cols'), may hold values from 0 to 1
- norm_gain: float32 [128], replicated, may hold values from 0.25 to 1.75
- norm_shift: float32 [128], replicated, may hold values from -3 to 3
- in_weight: bfloat16 [128, 512], replicated, may hold values from -1.5 to 1.5
- gate_bias: float32 [128], replicated, may hold values from -4 to 4
- bias_weight: bfloat16 [128, 4], replicated, may hold values from -16 to 16
- out_weight: bfloat16 [128, 128], replicated, may hold values from -1.5 to 1.5
- out_bias: float32 [128], replicated, may hold values from -1.8 to 1.8
Outputs:
- updated: bfloat16 [768, 768, 128], P('rows', 'cols')
The draws below stay inside these ranges and needn't reach their ends.
All inputs are finite; a program needn't handle non-finite values.
Results may differ from the reference program's by a relative error of at most 0.006.
The reference program's roundings to bfloat16 on the way count: a program that leaves them out, or rounds other values in their place, can miss the bound.
Values may be sent and summed in bfloat16 or wider, within the bound.
A program may use at most 128 MiB of HBM per device.

```python
import jax
import jax.numpy as jnp
from jax import lax

CHANNELS = 128
HEADS = 4
HEAD_DIM = 32
TOKENS = 768


def head_directions(key):
    return jax.random.normal(jax.random.fold_in(key, 11), (CHANNELS, HEADS), jnp.float32)


def channel_direction(key):
    return jax.random.normal(jax.random.fold_in(key, 31), (CHANNELS,), jnp.float32) / jnp.sqrt(jnp.float32(CHANNELS))


def head_coupling(key):
    signs = 2.0 * jax.random.randint(jax.random.fold_in(key, 32), (HEADS,), 0, 2).astype(jnp.float32) - 1.0
    sizes = jax.random.uniform(jax.random.fold_in(key, 33), (HEADS,), jnp.float32, 0.3, 0.5)
    return signs * sizes


def value_coupling(key):
    inner_width = HEADS * HEAD_DIM
    signs = 2.0 * jax.random.randint(jax.random.fold_in(key, 34), (inner_width,), 0, 2).astype(jnp.float32) - 1.0
    sizes = jax.random.uniform(jax.random.fold_in(key, 35), (inner_width,), jnp.float32, 0.7, 1.3)
    return signs * sizes


def draw_bias_weight(key, part):
    spread_part = head_directions(key) / jnp.sqrt(jnp.float32(CHANNELS))
    coupled = channel_direction(key)[:, None] * head_coupling(key)[None, :]
    base = 0.3 * spread_part + coupled
    return jnp.clip(base, -16.0, 16.0).astype(jnp.bfloat16)


def draw_in_weight(key, part):
    inner_width = HEADS * HEAD_DIM
    noise = jax.random.normal(jax.random.fold_in(key, 41), (CHANNELS, 4 * inner_width), jnp.float32)
    drawn = 1.0 / jnp.sqrt(jnp.float32(CHANNELS))
    front = drawn * jnp.ones((2 * inner_width,), jnp.float32)
    scales = jnp.concatenate((front, drawn * jnp.ones((2 * inner_width,), jnp.float32)))
    weight = noise * scales[None, :]
    coupling_row = jnp.concatenate((jnp.zeros((2 * inner_width,), jnp.float32), value_coupling(key), jnp.zeros((inner_width,), jnp.float32)))
    weight = weight + channel_direction(key)[:, None] * coupling_row[None, :]
    return jnp.clip(weight, -1.5, 1.5).astype(jnp.bfloat16)


def draw_pair(key, part):
    field = jax.random.normal(jax.random.fold_in(key, 5), (TOKENS, TOKENS, CHANNELS), jnp.float32)
    column_part = 1.5 * jax.random.normal(jax.random.fold_in(key, 36), (TOKENS,), jnp.float32)
    rough_part = 0.8 * jax.random.normal(jax.random.fold_in(key, 37), (TOKENS, TOKENS), jnp.float32)
    scalar_field = column_part[None, :] + rough_part
    field = field + scalar_field[:, :, None] * channel_direction(key)[None, None, :]
    return jnp.clip(field, -6.0, 6.0).astype(jnp.bfloat16)


def draw_token_mask(key, part):
    kept = (jax.random.randint(jax.random.fold_in(key, 23), (TOKENS,), 0, 32) != 0).astype(jnp.int32)
    anchor = jax.random.randint(jax.random.fold_in(key, 24), (), 0, TOKENS)
    missing = (anchor + jax.random.randint(jax.random.fold_in(key, 25), (), 1, TOKENS)) % TOKENS
    kept = kept.at[missing].set(0)
    return kept.at[anchor].set(1)


def scatter_about(own_key, extent, scale, limit, dtype=jnp.bfloat16):
    array = scale * jax.random.normal(own_key, extent, jnp.float32)
    return jnp.clip(array, min=-limit, max=limit).astype(dtype)


def setup_inputs(seed: int = 0) -> dict:
    key_list = jax.random.split(jax.random.key(seed), 10)
    pair = draw_pair(jax.random.fold_in(key_list[9], 71), 0)
    token_mask = draw_token_mask(jax.random.fold_in(key_list[9], 71), 0)
    norm_gain = jnp.clip(1.0 + 0.15 * jax.random.normal(key_list[2], (CHANNELS,), jnp.float32), 0.25, 1.75)
    norm_shift = scatter_about(key_list[3], (CHANNELS,), 0.5, 3.0, jnp.float32)
    in_weight = draw_in_weight(jax.random.fold_in(key_list[9], 71), 0)
    gate_bias = scatter_about(key_list[5], (HEADS * HEAD_DIM,), 1.0, 4.0, jnp.float32)
    bias_weight = draw_bias_weight(jax.random.fold_in(key_list[9], 71), 0)
    out_weight = scatter_about(key_list[7], (HEADS * HEAD_DIM, CHANNELS), 0.25, 1.5)
    out_bias = scatter_about(key_list[8], (CHANNELS,), 0.3, 1.8, jnp.float32)
    return {"pair": pair, "token_mask": token_mask, "norm_gain": norm_gain, "norm_shift": norm_shift, "in_weight": in_weight, "gate_bias": gate_bias, "bias_weight": bias_weight, "out_weight": out_weight, "out_bias": out_bias}


def layer_norm(pair_block, norm_gain, norm_shift):
    as_float = pair_block.astype(jnp.float32)
    center = lax.optimization_barrier(jnp.mean(as_float, axis=-1, keepdims=True))
    spread = lax.optimization_barrier(jnp.mean(jnp.square(as_float - center), axis=-1, keepdims=True))
    return ((as_float - center) * lax.rsqrt(spread + 1e-05) * norm_gain + norm_shift).astype(jnp.bfloat16)

def reference(pair, token_mask, norm_gain, norm_shift, in_weight, gate_bias, bias_weight, out_weight, out_bias):
    inner_width = HEADS * HEAD_DIM

    def bias_row(pair_row):
        normed = layer_norm(pair_row, norm_gain, norm_shift)
        return jnp.dot(normed, bias_weight, preferred_element_type=jnp.float32).astype(jnp.bfloat16)
    pair_bias = lax.map(bias_row, pair)
    bias_heads = jnp.transpose(pair_bias, (0, 2, 1)).astype(jnp.float32)
    masking = 1000000000.0 * (token_mask.astype(jnp.float32) - 1.0)

    def attend_row(pair_row):
        normed = layer_norm(pair_row, norm_gain, norm_shift)
        projected = jnp.dot(normed, in_weight, preferred_element_type=jnp.float32)
        queries = (projected[:, :inner_width] * HEAD_DIM ** (-0.5)).astype(jnp.bfloat16).reshape(TOKENS, HEADS, HEAD_DIM)
        keys_row = projected[:, inner_width:2 * inner_width].astype(jnp.bfloat16).reshape(TOKENS, HEADS, HEAD_DIM)
        values_row = projected[:, 2 * inner_width:3 * inner_width].astype(jnp.bfloat16).reshape(TOKENS, HEADS, HEAD_DIM)
        gates = jax.nn.sigmoid(projected[:, 3 * inner_width:] + gate_bias)
        scores = jnp.einsum('jhd,khd->jhk', queries.astype(jnp.float32), keys_row.astype(jnp.float32))
        scores = scores + bias_heads + masking
        top = lax.optimization_barrier(jnp.max(scores, axis=-1, keepdims=True))
        expo = jnp.exp(scores - top)
        totals = lax.optimization_barrier(jnp.sum(expo, axis=-1))
        weights = lax.optimization_barrier(expo.astype(jnp.bfloat16))
        summed = jnp.einsum('jhk,khd->jhd', weights.astype(jnp.float32), values_row.astype(jnp.float32))
        attended = summed / totals[..., None]
        gated = (gates * attended.reshape(TOKENS, inner_width)).astype(jnp.bfloat16)
        return (jnp.dot(gated, out_weight, preferred_element_type=jnp.float32) + out_bias).astype(jnp.bfloat16)
    return lax.map(attend_row, pair)
```

```python
import functools

import jax
import jax.numpy as jnp
from jax import lax
from jax.experimental import pallas as pl
from jax.experimental.pallas import tpu as pltpu
from jax.sharding import PartitionSpec as P


def layer_norm(pair_block, norm_gain, norm_shift):
    as_float = pair_block.astype(jnp.float32)
    center = jnp.mean(as_float, axis=-1, keepdims=True)
    spread = jnp.mean(jnp.square(as_float - center), axis=-1, keepdims=True)
    return ((as_float - center) * lax.rsqrt(spread + 1e-05) * norm_gain + norm_shift).astype(
        jnp.bfloat16
    )


def attend_kernel(
    head_count,
    head_size,
    own_ref,
    all_ref,
    bias_ref,
    mask_ref,
    wqg_ref,
    wkv_ref,
    gb_ref,
    ow_ref,
    ob_ref,
    out_ref,
):
    inner = head_count * head_size
    own = own_ref[0]
    qg = jnp.dot(own, wqg_ref[...], preferred_element_type=jnp.float32)
    queries = (qg[:, :inner] * head_size ** (-0.5)).astype(jnp.bfloat16)
    gates = jax.nn.sigmoid(qg[:, inner:] + gb_ref[...])
    row = all_ref[0]
    kv = jnp.dot(row, wkv_ref[...], preferred_element_type=jnp.float32)
    keys = kv[:, :inner].astype(jnp.bfloat16)
    values = kv[:, inner:].astype(jnp.bfloat16)
    lane_head = lax.broadcasted_iota(jnp.int32, (1, inner), 1) // head_size
    masking = mask_ref[...]
    attended = jnp.zeros((own.shape[0], inner), jnp.float32)
    for h in range(head_count):
        in_head = lane_head == h
        q_h = jnp.where(in_head, queries, jnp.zeros_like(queries))
        scores = lax.dot_general(
            q_h, keys, (((1,), (1,)), ((), ())), preferred_element_type=jnp.float32
        )
        scores = scores + bias_ref[h].astype(jnp.float32)
        scores = scores + masking
        top = jnp.max(scores, axis=-1, keepdims=True)
        expo = jnp.exp(scores - top)
        totals = jnp.sum(expo, axis=-1, keepdims=True)
        mixed = jnp.dot(expo.astype(jnp.bfloat16), values, preferred_element_type=jnp.float32)
        attended = jnp.where(in_head, mixed / totals, attended)
    gated = (gates * attended).astype(jnp.bfloat16)
    updated = jnp.dot(gated, ow_ref[...], preferred_element_type=jnp.float32) + ob_ref[...]
    out_ref[0] = updated.astype(out_ref.dtype)


def attend(normed, normed_all, bias, masking, wqg, wkv, gate_bias, out_weight, out_bias):
    row_count, col_count, channels = normed.shape
    span = normed_all.shape[1]
    head_count = bias.shape[0]
    inner = out_weight.shape[0]
    head_size = inner // head_count
    const2 = lambda i: (0, 0)
    return pl.pallas_call(
        functools.partial(attend_kernel, head_count, head_size),
        out_shape=jax.ShapeDtypeStruct((row_count, col_count, channels), jnp.bfloat16),
        grid=(row_count,),
        in_specs=[
            pl.BlockSpec((1, col_count, channels), lambda i: (i, 0, 0)),
            pl.BlockSpec((1, span, channels), lambda i: (i, 0, 0)),
            pl.BlockSpec((head_count, col_count, span), lambda i: (0, 0, 0)),
            pl.BlockSpec((1, span), const2),
            pl.BlockSpec(wqg.shape, const2),
            pl.BlockSpec(wkv.shape, const2),
            pl.BlockSpec((1, inner), const2),
            pl.BlockSpec(out_weight.shape, const2),
            pl.BlockSpec((1, channels), const2),
        ],
        out_specs=pl.BlockSpec((1, col_count, channels), lambda i: (i, 0, 0)),
    )(
        normed,
        normed_all,
        bias,
        masking,
        wqg,
        wkv,
        gate_bias.reshape(1, inner),
        out_weight,
        out_bias.reshape(1, channels),
    )


def shards(
    pair, token_mask, norm_gain, norm_shift, in_weight, gate_bias, bias_weight, out_weight, out_bias
):
    inner = out_weight.shape[0]
    normed = layer_norm(pair, norm_gain, norm_shift)
    bias_tile = jnp.einsum(
        "jkc,ch->hjk", normed, bias_weight, preferred_element_type=jnp.float32
    ).astype(jnp.bfloat16)
    bias_cols = lax.all_gather(bias_tile, "rows", axis=1, tiled=True)
    bias = lax.all_to_all(bias_cols, "cols", 1, 2, tiled=True)
    normed_all = lax.all_gather(normed, "cols", axis=1, tiled=True)
    mask_all = lax.all_gather(token_mask, "cols", axis=0, tiled=True)
    masking = (1000000000.0 * (mask_all.astype(jnp.float32) - 1.0)).reshape(1, -1)
    wqg = jnp.concatenate((in_weight[:, :inner], in_weight[:, 3 * inner :]), axis=1)
    wkv = in_weight[:, inner : 3 * inner]
    return attend(normed, normed_all, bias, masking, wqg, wkv, gate_bias, out_weight, out_bias)


def solution(mesh):
    placed = (P("rows", "cols", None), P("cols"), P(), P(), P(), P(), P(), P(), P())
    return jax.shard_map(
        shards, mesh=mesh, in_specs=placed, out_specs=P("rows", "cols", None), check_vma=False
    )
```

```python
import functools

import jax
import jax.numpy as jnp
from jax import lax
from jax.experimental import pallas as pl
from jax.experimental.pallas import tpu as pltpu
from jax.sharding import PartitionSpec as P


CHUNKS = 4


def layer_norm(pair_block, norm_gain, norm_shift):
    as_float = pair_block.astype(jnp.float32)
    center = jnp.mean(as_float, axis=-1, keepdims=True)
    spread = jnp.mean(jnp.square(as_float - center), axis=-1, keepdims=True)
    return ((as_float - center) * lax.rsqrt(spread + 1e-05) * norm_gain + norm_shift).astype(
        jnp.bfloat16
    )


def attend_kernel(
    head_count,
    head_size,
    own_ref,
    all_ref,
    bias_ref,
    wqg_ref,
    wkv_ref,
    gb_ref,
    ow_ref,
    ob_ref,
    out_ref,
):
    inner = head_count * head_size
    own = own_ref[0]
    qg = jnp.dot(own, wqg_ref[...], preferred_element_type=jnp.float32)
    queries = (qg[:, :inner] * head_size ** (-0.5)).astype(jnp.bfloat16)
    gates = jax.nn.sigmoid(qg[:, inner:] + gb_ref[...])
    row = all_ref[0]
    kv = jnp.dot(row, wkv_ref[...], preferred_element_type=jnp.float32)
    keys = kv[:, :inner].astype(jnp.bfloat16)
    values = kv[:, inner:].astype(jnp.bfloat16)
    lane_head = lax.broadcasted_iota(jnp.int32, (1, inner), 1) // head_size
    masking = 1000000000.0 * (bias_ref[head_count, 0:1, :].astype(jnp.float32) - 1.0)
    attended = jnp.zeros((own.shape[0], inner), jnp.float32)
    for h in range(head_count):
        in_head = lane_head == h
        q_h = jnp.where(in_head, queries, jnp.zeros_like(queries))
        scores = lax.dot_general(
            q_h, keys, (((1,), (1,)), ((), ())), preferred_element_type=jnp.float32
        )
        scores = scores + bias_ref[h].astype(jnp.float32)
        scores = scores + masking
        top = jnp.max(scores, axis=-1, keepdims=True)
        expo = jnp.exp(scores - top)
        totals = jnp.sum(expo, axis=-1, keepdims=True)
        mixed = jnp.dot(expo.astype(jnp.bfloat16), values, preferred_element_type=jnp.float32)
        attended = jnp.where(in_head, mixed / totals, attended)
    gated = (gates * attended).astype(jnp.bfloat16)
    updated = jnp.dot(gated, ow_ref[...], preferred_element_type=jnp.float32) + ob_ref[...]
    out_ref[0] = updated.astype(out_ref.dtype)


def attend(normed, normed_all, bias, wqg, wkv, gate_bias, out_weight, out_bias):
    row_count, col_count, channels = normed.shape
    span = normed_all.shape[1]
    head_count = bias.shape[0] - 1
    inner = out_weight.shape[0]
    head_size = inner // head_count
    const2 = lambda i: (0, 0)
    return pl.pallas_call(
        functools.partial(attend_kernel, head_count, head_size),
        out_shape=jax.ShapeDtypeStruct((row_count, col_count, channels), jnp.bfloat16),
        grid=(row_count,),
        in_specs=[
            pl.BlockSpec((1, col_count, channels), lambda i: (i, 0, 0)),
            pl.BlockSpec((1, span, channels), lambda i: (i, 0, 0)),
            pl.BlockSpec((head_count + 1, col_count, span), lambda i: (0, 0, 0)),
            pl.BlockSpec(wqg.shape, const2),
            pl.BlockSpec(wkv.shape, const2),
            pl.BlockSpec((1, inner), const2),
            pl.BlockSpec(out_weight.shape, const2),
            pl.BlockSpec((1, channels), const2),
        ],
        out_specs=pl.BlockSpec((1, col_count, channels), lambda i: (i, 0, 0)),
    )(
        normed,
        normed_all,
        bias,
        wqg,
        wkv,
        gate_bias.reshape(1, inner),
        out_weight,
        out_bias.reshape(1, channels),
    )


def shards(
    pair, token_mask, norm_gain, norm_shift, in_weight, gate_bias, bias_weight, out_weight, out_bias
):
    inner = out_weight.shape[0]
    normed = layer_norm(pair, norm_gain, norm_shift)
    bias_tile = jnp.einsum(
        "jkc,ch->hjk", normed, bias_weight, preferred_element_type=jnp.float32
    ).astype(jnp.bfloat16)
    mask_tile = jnp.broadcast_to(
        token_mask.astype(jnp.bfloat16)[None, None, :], (1,) + bias_tile.shape[1:]
    )
    payload = jnp.concatenate((bias_tile, mask_tile), axis=0)
    bias_cols = lax.all_gather(payload, "rows", axis=1, tiled=True)
    bias = lax.all_to_all(bias_cols, "cols", 1, 2, tiled=True)
    wqg = jnp.concatenate((in_weight[:, :inner], in_weight[:, 3 * inner :]), axis=1)
    wkv = in_weight[:, inner : 3 * inner]
    row_count = normed.shape[0]
    chunk = row_count // CHUNKS
    outs = []
    for q in range(CHUNKS):
        part = normed[q * chunk : (q + 1) * chunk]
        part_all = lax.all_gather(part, "cols", axis=1, tiled=True)
        outs.append(
            attend(part, part_all, bias, wqg, wkv, gate_bias, out_weight, out_bias)
        )
    return jnp.concatenate(outs, axis=0)


def solution(mesh):
    placed = (P("rows", "cols", None), P("cols"), P(), P(), P(), P(), P(), P(), P())
    return jax.shard_map(
        shards, mesh=mesh, in_specs=placed, out_specs=P("rows", "cols", None), check_vma=False
    )
```

```python
import functools

import jax
import jax.numpy as jnp
from jax import lax
from jax.experimental import pallas as pl
from jax.experimental.pallas import tpu as pltpu
from jax.sharding import PartitionSpec as P


def layer_norm(pair_block, norm_gain, norm_shift):
    as_float = pair_block.astype(jnp.float32)
    center = jnp.mean(as_float, axis=-1, keepdims=True)
    spread = jnp.mean(jnp.square(as_float - center), axis=-1, keepdims=True)
    return ((as_float - center) * lax.rsqrt(spread + 1e-05) * norm_gain + norm_shift).astype(
        jnp.bfloat16
    )


def attend_kernel(
    head_count,
    head_size,
    own_ref,
    all_ref,
    bias_ref,
    wqg_ref,
    wkv_ref,
    gb_ref,
    ow_ref,
    ob_ref,
    out_ref,
):
    inner = head_count * head_size
    own = own_ref[0]
    qg = jnp.dot(own, wqg_ref[...], preferred_element_type=jnp.float32)
    queries = (qg[:, :inner] * head_size ** (-0.5)).astype(jnp.bfloat16)
    gates = jax.nn.sigmoid(qg[:, inner:] + gb_ref[...])
    row = all_ref[0]
    kv = jnp.dot(row, wkv_ref[...], preferred_element_type=jnp.float32)
    keys = kv[:, :inner].astype(jnp.bfloat16)
    values = kv[:, inner:].astype(jnp.bfloat16)
    lane_head = lax.broadcasted_iota(jnp.int32, (1, inner), 1) // head_size
    masking = 1000000000.0 * (bias_ref[head_count, 0:1, :].astype(jnp.float32) - 1.0)
    attended = jnp.zeros((own.shape[0], inner), jnp.float32)
    for h in range(head_count):
        in_head = lane_head == h
        q_h = jnp.where(in_head, queries, jnp.zeros_like(queries))
        scores = lax.dot_general(
            q_h, keys, (((1,), (1,)), ((), ())), preferred_element_type=jnp.float32
        )
        scores = scores + bias_ref[h].astype(jnp.float32)
        scores = scores + masking
        top = jnp.max(scores, axis=-1, keepdims=True)
        expo = jnp.exp(scores - top)
        totals = jnp.sum(expo, axis=-1, keepdims=True)
        mixed = jnp.dot(expo.astype(jnp.bfloat16), values, preferred_element_type=jnp.float32)
        attended = jnp.where(in_head, mixed / totals, attended)
    gated = (gates * attended).astype(jnp.bfloat16)
    updated = jnp.dot(gated, ow_ref[...], preferred_element_type=jnp.float32) + ob_ref[...]
    out_ref[0] = updated.astype(out_ref.dtype)


def attend(normed, normed_all, bias, wqg, wkv, gate_bias, out_weight, out_bias):
    row_count, col_count, channels = normed.shape
    span = normed_all.shape[1]
    head_count = bias.shape[0] - 1
    inner = out_weight.shape[0]
    head_size = inner // head_count
    const2 = lambda i: (0, 0)
    return pl.pallas_call(
        functools.partial(attend_kernel, head_count, head_size),
        out_shape=jax.ShapeDtypeStruct((row_count, col_count, channels), jnp.bfloat16),
        grid=(row_count,),
        in_specs=[
            pl.BlockSpec((1, col_count, channels), lambda i: (i, 0, 0)),
            pl.BlockSpec((1, span, channels), lambda i: (i, 0, 0)),
            pl.BlockSpec((head_count + 1, col_count, span), lambda i: (0, 0, 0)),
            pl.BlockSpec(wqg.shape, const2),
            pl.BlockSpec(wkv.shape, const2),
            pl.BlockSpec((1, inner), const2),
            pl.BlockSpec(out_weight.shape, const2),
            pl.BlockSpec((1, channels), const2),
        ],
        out_specs=pl.BlockSpec((1, col_count, channels), lambda i: (i, 0, 0)),
    )(
        normed,
        normed_all,
        bias,
        wqg,
        wkv,
        gate_bias.reshape(1, inner),
        out_weight,
        out_bias.reshape(1, channels),
    )


def exchange_kernel(normed_ref, payload_ref, all_ref, bias_ref, norm_send, norm_recv, bias_send, bias_recv, local_sem):
    col_count = lax.axis_size("cols")
    row_count = lax.axis_size("rows")
    group = row_count // col_count
    me_r = lax.axis_index("rows")
    me_c = lax.axis_index("cols")
    width = normed_ref.shape[1]
    home = pl.ds(pl.multiple_of(me_c * width, width), width)
    mesh_id = pl.DeviceIdType.MESH
    copies = []
    local = pltpu.make_async_copy(normed_ref, all_ref.at[:, home, :], local_sem.at[0])
    local.start()
    for p in range(1, col_count):
        peer = lax.rem(me_c + p, col_count)
        copy = pltpu.make_async_remote_copy(
            src_ref=normed_ref,
            dst_ref=all_ref.at[:, home, :],
            send_sem=norm_send.at[p],
            recv_sem=norm_recv,
            device_id=(me_r, peer),
            device_id_type=mesh_id,
        )
        copy.start()
        copies.append(copy)
    target_c = me_r // group
    slot = me_c * group + lax.rem(me_r, group)
    self_slot = (target_c == me_c)
    local_bias = pltpu.make_async_copy(payload_ref, bias_ref.at[slot], bias_recv)
    bias_copies = []
    for r in range(row_count):
        is_self = jnp.logical_and(self_slot, me_r == r)
        copy = pltpu.make_async_remote_copy(
            src_ref=payload_ref,
            dst_ref=bias_ref.at[slot],
            send_sem=bias_send.at[r],
            recv_sem=bias_recv,
            device_id=(r, target_c),
            device_id_type=mesh_id,
        )

        @pl.when(jnp.logical_not(is_self))
        def _():
            copy.start()

        @pl.when(is_self)
        def _():
            local_bias.start()

        bias_copies.append((is_self, copy))
    local.wait()
    for copy in copies:
        copy.wait_send()
    pltpu.make_async_copy(
        all_ref.at[:, pl.ds(0, (col_count - 1) * width), :],
        all_ref.at[:, pl.ds(0, (col_count - 1) * width), :],
        norm_recv,
    ).wait()
    for is_self, copy in bias_copies:

        @pl.when(jnp.logical_not(is_self))
        def _():
            copy.wait_send()

    pltpu.make_async_copy(bias_ref, bias_ref, bias_recv).wait()


def exchange(normed, payload):
    row_count, col_count, channels = normed.shape
    cols = lax.axis_size("cols")
    rows = lax.axis_size("rows")
    any_spec = pl.BlockSpec(memory_space=pl.ANY)
    return pl.pallas_call(
        exchange_kernel,
        out_shape=(
            jax.ShapeDtypeStruct((row_count, cols * col_count, channels), normed.dtype),
            jax.ShapeDtypeStruct((rows,) + payload.shape, payload.dtype),
        ),
        in_specs=[any_spec, any_spec],
        out_specs=(any_spec, any_spec),
        scratch_shapes=[
            pltpu.SemaphoreType.DMA((cols,)),
            pltpu.SemaphoreType.DMA(()),
            pltpu.SemaphoreType.DMA((rows,)),
            pltpu.SemaphoreType.DMA(()),
            pltpu.SemaphoreType.DMA((1,)),
        ],
        compiler_params=pltpu.CompilerParams(has_side_effects=True),
    )(normed, payload)


def shards(
    pair, token_mask, norm_gain, norm_shift, in_weight, gate_bias, bias_weight, out_weight, out_bias
):
    inner = out_weight.shape[0]
    normed = layer_norm(pair, norm_gain, norm_shift)
    bias_tile = jnp.einsum(
        "jkc,ch->hjk", normed, bias_weight, preferred_element_type=jnp.float32
    ).astype(jnp.bfloat16)
    mask_tile = jnp.broadcast_to(
        token_mask.astype(jnp.bfloat16)[None, None, :], (1,) + bias_tile.shape[1:]
    )
    payload = jnp.concatenate((bias_tile, mask_tile), axis=0)
    normed_all, bias_in = exchange(normed, payload)
    cols = lax.axis_size("cols")
    group = lax.axis_size("rows") // cols
    slots, width = payload.shape[0], payload.shape[2]
    bias = bias_in.reshape(cols, group, slots, payload.shape[1], width)
    bias = jnp.transpose(bias, (2, 1, 3, 0, 4)).reshape(
        slots, group * payload.shape[1], cols * width
    )
    wqg = jnp.concatenate((in_weight[:, :inner], in_weight[:, 3 * inner :]), axis=1)
    wkv = in_weight[:, inner : 3 * inner]
    return attend(normed, normed_all, bias, wqg, wkv, gate_bias, out_weight, out_bias)


def solution(mesh):
    placed = (P("rows", "cols", None), P("cols"), P(), P(), P(), P(), P(), P(), P())
    return jax.shard_map(
        shards, mesh=mesh, in_specs=placed, out_specs=P("rows", "cols", None), check_vma=False
    )
```

```python
import functools

import jax
import jax.numpy as jnp
from jax import lax
from jax.experimental import pallas as pl
from jax.experimental.pallas import tpu as pltpu
from jax.sharding import PartitionSpec as P


def layer_norm(pair_block, norm_gain, norm_shift):
    as_float = pair_block.astype(jnp.float32)
    center = jnp.mean(as_float, axis=-1, keepdims=True)
    spread = jnp.mean(jnp.square(as_float - center), axis=-1, keepdims=True)
    return ((as_float - center) * lax.rsqrt(spread + 1e-05) * norm_gain + norm_shift).astype(
        jnp.bfloat16
    )


CHUNKS = 4


def row_update(own, row, bias_ref, masking, wqg, wkv, gb, ow, ob, head_count, head_size):
    inner = head_count * head_size
    qg = jnp.dot(own, wqg, preferred_element_type=jnp.float32)
    queries = (qg[:, :inner] * head_size ** (-0.5)).astype(jnp.bfloat16)
    gates = jax.nn.sigmoid(qg[:, inner:] + gb)
    kv = jnp.dot(row, wkv, preferred_element_type=jnp.float32)
    keys = kv[:, :inner].astype(jnp.bfloat16)
    values = kv[:, inner:].astype(jnp.bfloat16)
    lane_head = lax.broadcasted_iota(jnp.int32, (1, inner), 1) // head_size
    attended = jnp.zeros((own.shape[0], inner), jnp.float32)
    for h in range(head_count):
        in_head = lane_head == h
        q_h = jnp.where(in_head, queries, jnp.zeros_like(queries))
        scores = lax.dot_general(
            q_h, keys, (((1,), (1,)), ((), ())), preferred_element_type=jnp.float32
        )
        scores = scores + bias_ref[h]
        scores = scores + masking
        top = jnp.max(scores, axis=-1, keepdims=True)
        expo = jnp.exp(scores - top)
        totals = jnp.sum(expo, axis=-1, keepdims=True)
        mixed = jnp.dot(expo.astype(jnp.bfloat16), values, preferred_element_type=jnp.float32)
        attended = jnp.where(in_head, mixed / totals, attended)
    gated = (gates * attended).astype(jnp.bfloat16)
    return jnp.dot(gated, ow, preferred_element_type=jnp.float32) + ob


def fused_kernel(
    head_count,
    own_ref,
    pay_ref,
    wqg_ref,
    wkv_ref,
    gb_ref,
    ow_ref,
    ob_ref,
    out_ref,
    rows_buf,
    pieces,
    bias_buf,
    norm_send,
    norm_recv,
    local_sem,
    bias_send,
    bias_recv,
):
    col_count = lax.axis_size("cols")
    row_count = lax.axis_size("rows")
    group = row_count // col_count
    me_r = lax.axis_index("rows")
    me_c = lax.axis_index("cols")
    own_rows, width, channels = own_ref.shape
    depth = pay_ref.shape[1]
    chunk = own_rows // CHUNKS
    mesh_id = pl.DeviceIdType.MESH
    target_c = me_r // group
    is_home = target_c == me_c
    barrier = pltpu.get_barrier_semaphore()
    for p in range(1, col_count):
        pl.semaphore_signal(
            barrier, 1, device_id=(me_r, lax.rem(me_c + p, col_count)), device_id_type=mesh_id
        )
    for r in range(row_count):

        @pl.when(jnp.logical_not(jnp.logical_and(is_home, me_r == r)))
        def _():
            pl.semaphore_signal(barrier, 1, device_id=(r, target_c), device_id_type=mesh_id)

    for m in range(group):
        for c in range(col_count):

            @pl.when(jnp.logical_not(jnp.logical_and(group * me_c + m == me_r, me_c == c)))
            def _():
                pl.semaphore_signal(
                    barrier, 1, device_id=(group * me_c + m, c), device_id_type=mesh_id
                )

    pl.semaphore_wait(barrier, col_count - 1 + 2 * (row_count - is_home.astype(jnp.int32)))

    slot = me_c * group + lax.rem(me_r, group)
    local_bias = pltpu.make_async_copy(pay_ref, pieces.at[slot], bias_recv)
    bias_copies = []
    for r in range(row_count):
        is_self = jnp.logical_and(is_home, me_r == r)
        copy = pltpu.make_async_remote_copy(
            src_ref=pay_ref,
            dst_ref=pieces.at[slot],
            send_sem=bias_send.at[r],
            recv_sem=bias_recv,
            device_id=(r, target_c),
            device_id_type=mesh_id,
        )

        @pl.when(jnp.logical_not(is_self))
        def _():
            copy.start()

        @pl.when(is_self)
        def _():
            local_bias.start()

        bias_copies.append((is_self, copy))

    home = pl.ds(pl.multiple_of(me_c * width, width), width)
    norm_copies = []
    locals_ = []
    for q in range(CHUNKS):
        part = pl.ds(q * chunk, chunk)
        local = pltpu.make_async_copy(own_ref.at[part], rows_buf.at[part, home, :], local_sem.at[q])
        local.start()
        locals_.append(local)
        for p in range(1, col_count):
            copy = pltpu.make_async_remote_copy(
                src_ref=own_ref.at[part],
                dst_ref=rows_buf.at[part, home, :],
                send_sem=norm_send.at[q, p],
                recv_sem=norm_recv.at[q],
                device_id=(me_r, lax.rem(me_c + p, col_count)),
                device_id_type=mesh_id,
            )
            copy.start()
            norm_copies.append(copy)

    pltpu.make_async_copy(pieces, pieces, bias_recv).wait()
    for c in range(col_count):
        for m in range(group):
            bias_buf[:, m * depth : (m + 1) * depth, c * width : (c + 1) * width] = pieces[
                c * group + m
            ].astype(jnp.float32)
    masking = 1000000000.0 * (bias_buf[head_count, 0:1, :] - 1.0)
    inner = ow_ref.shape[0]
    head_size = inner // head_count

    for q in range(CHUNKS):
        locals_[q].wait()
        arrived = pl.ds(0, (col_count - 1) * width)
        pltpu.make_async_copy(
            rows_buf.at[pl.ds(q * chunk, chunk), arrived, :],
            rows_buf.at[pl.ds(q * chunk, chunk), arrived, :],
            norm_recv.at[q],
        ).wait()

        def body(i, carry):
            updated = row_update(
                own_ref[i],
                rows_buf[i],
                bias_buf,
                masking,
                wqg_ref[...],
                wkv_ref[...],
                gb_ref[...],
                ow_ref[...],
                ob_ref[...],
                head_count,
                head_size,
            )
            out_ref[i] = updated.astype(out_ref.dtype)
            return carry

        lax.fori_loop(q * chunk, (q + 1) * chunk, body, 0)

    for copy in norm_copies:
        copy.wait_send()
    for is_self, copy in bias_copies:

        @pl.when(jnp.logical_not(is_self))
        def _():
            copy.wait_send()


def fused(normed, payload, wqg, wkv, gate_bias, out_weight, out_bias):
    own_rows, width, channels = normed.shape
    cols = lax.axis_size("cols")
    rows = lax.axis_size("rows")
    slots, depth, _ = payload.shape
    group = rows // cols
    inner = out_weight.shape[0]
    vmem = pl.BlockSpec(memory_space=pltpu.VMEM)
    return pl.pallas_call(
        functools.partial(fused_kernel, slots - 1),
        out_shape=jax.ShapeDtypeStruct(normed.shape, jnp.bfloat16),
        in_specs=[vmem] * 7,
        out_specs=vmem,
        scratch_shapes=[
            pltpu.VMEM((own_rows, cols * width, channels), normed.dtype),
            pltpu.VMEM((rows,) + payload.shape, payload.dtype),
            pltpu.VMEM((slots, group * depth, cols * width), jnp.float32),
            pltpu.SemaphoreType.DMA((CHUNKS, cols)),
            pltpu.SemaphoreType.DMA((CHUNKS,)),
            pltpu.SemaphoreType.DMA((CHUNKS,)),
            pltpu.SemaphoreType.DMA((rows,)),
            pltpu.SemaphoreType.DMA(()),
        ],
        compiler_params=pltpu.CompilerParams(
            has_side_effects=True, collective_id=0, vmem_limit_bytes=48 * 1024 * 1024
        ),
    )(
        normed,
        payload,
        wqg,
        wkv,
        gate_bias.reshape(1, inner),
        out_weight,
        out_bias.reshape(1, channels),
    )


def shards(
    pair, token_mask, norm_gain, norm_shift, in_weight, gate_bias, bias_weight, out_weight, out_bias
):
    inner = out_weight.shape[0]
    normed = layer_norm(pair, norm_gain, norm_shift)
    bias_tile = jnp.einsum(
        "jkc,ch->hjk", normed, bias_weight, preferred_element_type=jnp.float32
    ).astype(jnp.bfloat16)
    mask_tile = jnp.broadcast_to(
        token_mask.astype(jnp.bfloat16)[None, None, :], (1,) + bias_tile.shape[1:]
    )
    payload = jnp.concatenate((bias_tile, mask_tile), axis=0)
    wqg = jnp.concatenate((in_weight[:, :inner], in_weight[:, 3 * inner :]), axis=1)
    wkv = in_weight[:, inner : 3 * inner]
    return fused(normed, payload, wqg, wkv, gate_bias, out_weight, out_bias)


def solution(mesh):
    placed = (P("rows", "cols", None), P("cols"), P(), P(), P(), P(), P(), P(), P())
    return jax.shard_map(
        shards, mesh=mesh, in_specs=placed, out_specs=P("rows", "cols", None), check_vma=False
    )
```

```python
import functools

import jax
import jax.numpy as jnp
from jax import lax
from jax.experimental import pallas as pl
from jax.experimental.pallas import tpu as pltpu
from jax.sharding import PartitionSpec as P


def layer_norm(pair_block, norm_gain, norm_shift):
    as_float = pair_block.astype(jnp.float32)
    center = jnp.mean(as_float, axis=-1, keepdims=True)
    spread = jnp.mean(jnp.square(as_float - center), axis=-1, keepdims=True)
    return ((as_float - center) * lax.rsqrt(spread + 1e-05) * norm_gain + norm_shift).astype(
        jnp.bfloat16
    )


CHUNKS = 4


def row_update(own, row, bias_ref, masking, wqg, wkv, gb, ow, ob, head_count, head_size):
    inner = head_count * head_size
    qg = jnp.dot(own, wqg, preferred_element_type=jnp.float32)
    queries = (qg[:, :inner] * head_size ** (-0.5)).astype(jnp.bfloat16)
    gates = jax.nn.sigmoid(qg[:, inner:] + gb)
    keys_t = lax.dot_general(
        wkv[:, :inner], row, (((0,), (1,)), ((), ())), preferred_element_type=jnp.float32
    ).astype(jnp.bfloat16)
    values = jnp.dot(row, wkv[:, inner:], preferred_element_type=jnp.float32).astype(jnp.bfloat16)
    lane_head = lax.broadcasted_iota(jnp.int32, (1, inner), 1) // head_size
    attended = jnp.zeros((own.shape[0], inner), jnp.float32)
    for h in range(head_count):
        in_head = lane_head == h
        q_h = jnp.where(in_head, queries, jnp.zeros_like(queries))
        scores = jnp.dot(q_h, keys_t, preferred_element_type=jnp.float32)
        scores = scores + bias_ref[h]
        scores = scores + masking
        top = jnp.max(scores, axis=-1, keepdims=True)
        expo = jnp.exp(scores - top)
        totals = jnp.sum(expo, axis=-1, keepdims=True)
        mixed = jnp.dot(expo.astype(jnp.bfloat16), values, preferred_element_type=jnp.float32)
        attended = jnp.where(in_head, mixed / totals, attended)
    gated = (gates * attended).astype(jnp.bfloat16)
    return jnp.dot(gated, ow, preferred_element_type=jnp.float32) + ob


def fused_kernel(
    head_count,
    own_ref,
    pay_ref,
    wqg_ref,
    wkv_ref,
    gb_ref,
    ow_ref,
    ob_ref,
    out_ref,
    rows_buf,
    pieces,
    bias_buf,
    norm_send,
    norm_recv,
    local_sem,
    bias_send,
    bias_recv,
):
    col_count = lax.axis_size("cols")
    row_count = lax.axis_size("rows")
    group = row_count // col_count
    me_r = lax.axis_index("rows")
    me_c = lax.axis_index("cols")
    own_rows, width, channels = own_ref.shape
    depth = pay_ref.shape[1]
    chunk = own_rows // CHUNKS
    mesh_id = pl.DeviceIdType.MESH
    target_c = me_r // group
    is_home = target_c == me_c
    barrier = pltpu.get_barrier_semaphore()
    for p in range(1, col_count):
        pl.semaphore_signal(
            barrier, 1, device_id=(me_r, lax.rem(me_c + p, col_count)), device_id_type=mesh_id
        )
    for r in range(row_count):

        @pl.when(jnp.logical_not(jnp.logical_and(is_home, me_r == r)))
        def _():
            pl.semaphore_signal(barrier, 1, device_id=(r, target_c), device_id_type=mesh_id)

    for m in range(group):
        for c in range(col_count):

            @pl.when(jnp.logical_not(jnp.logical_and(group * me_c + m == me_r, me_c == c)))
            def _():
                pl.semaphore_signal(
                    barrier, 1, device_id=(group * me_c + m, c), device_id_type=mesh_id
                )

    pl.semaphore_wait(barrier, col_count - 1 + 2 * (row_count - is_home.astype(jnp.int32)))

    slot = me_c * group + lax.rem(me_r, group)
    local_bias = pltpu.make_async_copy(pay_ref, pieces.at[slot], bias_recv)
    bias_copies = []
    for r in range(row_count):
        is_self = jnp.logical_and(is_home, me_r == r)
        copy = pltpu.make_async_remote_copy(
            src_ref=pay_ref,
            dst_ref=pieces.at[slot],
            send_sem=bias_send.at[r],
            recv_sem=bias_recv,
            device_id=(r, target_c),
            device_id_type=mesh_id,
        )

        @pl.when(jnp.logical_not(is_self))
        def _():
            copy.start()

        @pl.when(is_self)
        def _():
            local_bias.start()

        bias_copies.append((is_self, copy))

    home = pl.ds(pl.multiple_of(me_c * width, width), width)
    norm_copies = []
    locals_ = []
    for q in range(CHUNKS):
        part = pl.ds(q * chunk, chunk)
        local = pltpu.make_async_copy(own_ref.at[part], rows_buf.at[part, home, :], local_sem.at[q])
        local.start()
        locals_.append(local)
        for p in range(1, col_count):
            copy = pltpu.make_async_remote_copy(
                src_ref=own_ref.at[part],
                dst_ref=rows_buf.at[part, home, :],
                send_sem=norm_send.at[q, p],
                recv_sem=norm_recv.at[q],
                device_id=(me_r, lax.rem(me_c + p, col_count)),
                device_id_type=mesh_id,
            )
            copy.start()
            norm_copies.append(copy)

    pltpu.make_async_copy(pieces, pieces, bias_recv).wait()
    for c in range(col_count):
        for m in range(group):
            bias_buf[:, m * depth : (m + 1) * depth, c * width : (c + 1) * width] = pieces[
                c * group + m
            ].astype(jnp.float32)
    masking = 1000000000.0 * (bias_buf[head_count, 0:1, :] - 1.0)
    inner = ow_ref.shape[0]
    head_size = inner // head_count

    for q in range(CHUNKS):
        locals_[q].wait()
        arrived = pl.ds(0, (col_count - 1) * width)
        pltpu.make_async_copy(
            rows_buf.at[pl.ds(q * chunk, chunk), arrived, :],
            rows_buf.at[pl.ds(q * chunk, chunk), arrived, :],
            norm_recv.at[q],
        ).wait()

        def body(i, carry):
            updated = row_update(
                own_ref[i],
                rows_buf[i],
                bias_buf,
                masking,
                wqg_ref[...],
                wkv_ref[...],
                gb_ref[...],
                ow_ref[...],
                ob_ref[...],
                head_count,
                head_size,
            )
            out_ref[i] = updated.astype(out_ref.dtype)
            return carry

        lax.fori_loop(q * chunk, (q + 1) * chunk, body, 0)

    for copy in norm_copies:
        copy.wait_send()
    for is_self, copy in bias_copies:

        @pl.when(jnp.logical_not(is_self))
        def _():
            copy.wait_send()


def fused(normed, payload, wqg, wkv, gate_bias, out_weight, out_bias):
    own_rows, width, channels = normed.shape
    cols = lax.axis_size("cols")
    rows = lax.axis_size("rows")
    slots, depth, _ = payload.shape
    group = rows // cols
    inner = out_weight.shape[0]
    vmem = pl.BlockSpec(memory_space=pltpu.VMEM)
    return pl.pallas_call(
        functools.partial(fused_kernel, slots - 1),
        out_shape=jax.ShapeDtypeStruct(normed.shape, jnp.bfloat16),
        in_specs=[vmem] * 7,
        out_specs=vmem,
        scratch_shapes=[
            pltpu.VMEM((own_rows, cols * width, channels), normed.dtype),
            pltpu.VMEM((rows,) + payload.shape, payload.dtype),
            pltpu.VMEM((slots, group * depth, cols * width), jnp.float32),
            pltpu.SemaphoreType.DMA((CHUNKS, cols)),
            pltpu.SemaphoreType.DMA((CHUNKS,)),
            pltpu.SemaphoreType.DMA((CHUNKS,)),
            pltpu.SemaphoreType.DMA((rows,)),
            pltpu.SemaphoreType.DMA(()),
        ],
        compiler_params=pltpu.CompilerParams(
            has_side_effects=True, collective_id=0, vmem_limit_bytes=48 * 1024 * 1024
        ),
    )(
        normed,
        payload,
        wqg,
        wkv,
        gate_bias.reshape(1, inner),
        out_weight,
        out_bias.reshape(1, channels),
    )


def shards(
    pair, token_mask, norm_gain, norm_shift, in_weight, gate_bias, bias_weight, out_weight, out_bias
):
    inner = out_weight.shape[0]
    normed = layer_norm(pair, norm_gain, norm_shift)
    bias_tile = jnp.einsum(
        "jkc,ch->hjk", normed, bias_weight, preferred_element_type=jnp.float32
    ).astype(jnp.bfloat16)
    mask_tile = jnp.broadcast_to(
        token_mask.astype(jnp.bfloat16)[None, None, :], (1,) + bias_tile.shape[1:]
    )
    payload = jnp.concatenate((bias_tile, mask_tile), axis=0)
    wqg = jnp.concatenate((in_weight[:, :inner], in_weight[:, 3 * inner :]), axis=1)
    wkv = in_weight[:, inner : 3 * inner]
    return fused(normed, payload, wqg, wkv, gate_bias, out_weight, out_bias)


def solution(mesh):
    placed = (P("rows", "cols", None), P("cols"), P(), P(), P(), P(), P(), P(), P())
    return jax.shard_map(
        shards, mesh=mesh, in_specs=placed, out_specs=P("rows", "cols", None), check_vma=False
    )
```

```python
import functools

import jax
import jax.numpy as jnp
from jax import lax
from jax.experimental import pallas as pl
from jax.experimental.pallas import tpu as pltpu
from jax.sharding import PartitionSpec as P


def layer_norm(pair_block, norm_gain, norm_shift):
    as_float = pair_block.astype(jnp.float32)
    center = jnp.mean(as_float, axis=-1, keepdims=True)
    spread = jnp.mean(jnp.square(as_float - center), axis=-1, keepdims=True)
    return ((as_float - center) * lax.rsqrt(spread + 1e-05) * norm_gain + norm_shift).astype(
        jnp.bfloat16
    )


CHUNKS = 4


def row_update(own, row, bias_ref, masking, wqg, wkv, gb, ow, ob, head_count, head_size):
    inner = head_count * head_size
    qg = jnp.dot(own, wqg, preferred_element_type=jnp.float32)
    queries = (qg[:, :inner] * head_size ** (-0.5)).astype(jnp.bfloat16)
    gates = jax.nn.sigmoid(qg[:, inner:] + gb)
    keys_t = lax.dot_general(
        wkv[:, :inner], row, (((0,), (1,)), ((), ())), preferred_element_type=jnp.float32
    ).astype(jnp.bfloat16)
    values = jnp.dot(row, wkv[:, inner:], preferred_element_type=jnp.float32).astype(jnp.bfloat16)
    lane_head = lax.broadcasted_iota(jnp.int32, (1, inner), 1) // head_size
    attended = jnp.zeros((own.shape[0], inner), jnp.float32)
    for h in range(head_count):
        in_head = lane_head == h
        q_h = jnp.where(in_head, queries, jnp.zeros_like(queries))
        scores = jnp.dot(q_h, keys_t, preferred_element_type=jnp.float32)
        scores = scores + bias_ref[h]
        scores = scores + masking
        top = jnp.max(scores, axis=-1, keepdims=True)
        expo = jnp.exp(scores - top)
        totals = jnp.sum(expo, axis=-1, keepdims=True)
        mixed = jnp.dot(expo.astype(jnp.bfloat16), values, preferred_element_type=jnp.float32)
        attended = jnp.where(in_head, mixed / totals, attended)
    gated = (gates * attended).astype(jnp.bfloat16)
    return jnp.dot(gated, ow, preferred_element_type=jnp.float32) + ob


def fused_kernel(
    head_count,
    own_ref,
    pay_ref,
    wqg_ref,
    wkv_ref,
    gb_ref,
    ow_ref,
    ob_ref,
    out_ref,
    rows_buf,
    pieces,
    bias_buf,
    norm_send,
    norm_recv,
    local_sem,
    bias_send,
    bias_recv,
    fwd_sem,
):
    col_count = lax.axis_size("cols")
    row_count = lax.axis_size("rows")
    group = row_count // col_count
    me_r = lax.axis_index("rows")
    me_c = lax.axis_index("cols")
    own_rows, width, channels = own_ref.shape
    depth = pay_ref.shape[1]
    chunk = own_rows // CHUNKS
    mesh_id = pl.DeviceIdType.MESH
    target_c = me_r // group
    is_home = target_c == me_c
    parity = lax.rem(me_r, 2)
    half = row_count // 2
    sibling = me_r + 1 - 2 * parity
    barrier = pltpu.get_barrier_semaphore()
    for p in range(1, col_count):
        pl.semaphore_signal(
            barrier, 1, device_id=(me_r, lax.rem(me_c + p, col_count)), device_id_type=mesh_id
        )
    pl.semaphore_signal(barrier, 1, device_id=(sibling, me_c), device_id_type=mesh_id)
    for t in range(half):
        r = 2 * t + parity

        @pl.when(jnp.logical_not(jnp.logical_and(is_home, me_r == r)))
        def _():
            pl.semaphore_signal(barrier, 1, device_id=(r, target_c), device_id_type=mesh_id)

    for u in range(group // 2):
        for c in range(col_count):
            source = group * me_c + 2 * u + parity

            @pl.when(jnp.logical_not(jnp.logical_and(source == me_r, me_c == c)))
            def _():
                pl.semaphore_signal(barrier, 1, device_id=(source, c), device_id_type=mesh_id)

    pl.semaphore_wait(barrier, col_count + 2 * (half - is_home.astype(jnp.int32)))

    block = lax.rem(me_r, group)
    slot = lax.rem(block, 2) * half + (block // 2) * col_count + me_c
    local_bias = pltpu.make_async_copy(pay_ref, pieces.at[slot], bias_recv)
    bias_copies = []
    for t in range(half):
        r = 2 * t + parity
        is_self = jnp.logical_and(is_home, me_r == r)
        copy = pltpu.make_async_remote_copy(
            src_ref=pay_ref,
            dst_ref=pieces.at[slot],
            send_sem=bias_send.at[t],
            recv_sem=bias_recv,
            device_id=(r, target_c),
            device_id_type=mesh_id,
        )

        @pl.when(jnp.logical_not(is_self))
        def _():
            copy.start()

        @pl.when(is_self)
        def _():
            local_bias.start()

        bias_copies.append((is_self, copy))

    home = pl.ds(pl.multiple_of(me_c * width, width), width)
    norm_copies = []
    locals_ = []
    for q in range(CHUNKS):
        part = pl.ds(q * chunk, chunk)
        local = pltpu.make_async_copy(own_ref.at[part], rows_buf.at[part, home, :], local_sem.at[q])
        local.start()
        locals_.append(local)
        for p in range(1, col_count):
            copy = pltpu.make_async_remote_copy(
                src_ref=own_ref.at[part],
                dst_ref=rows_buf.at[part, home, :],
                send_sem=norm_send.at[q, p],
                recv_sem=norm_recv.at[q],
                device_id=(me_r, lax.rem(me_c + p, col_count)),
                device_id_type=mesh_id,
            )
            copy.start()
            norm_copies.append(copy)

    direct = pieces.at[pl.ds(pl.multiple_of(parity * half, half), half)]
    pltpu.make_async_copy(direct, direct, bias_recv).wait()
    forward = pltpu.make_async_remote_copy(
        src_ref=direct,
        dst_ref=direct,
        send_sem=fwd_sem.at[0],
        recv_sem=fwd_sem.at[1],
        device_id=(sibling, me_c),
        device_id_type=mesh_id,
    )
    forward.start()
    forward.wait()
    for c in range(col_count):
        for m in range(group):
            bias_buf[:, m * depth : (m + 1) * depth, c * width : (c + 1) * width] = pieces[
                (m % 2) * half + (m // 2) * col_count + c
            ].astype(jnp.float32)
    masking = 1000000000.0 * (bias_buf[head_count, 0:1, :] - 1.0)
    inner = ow_ref.shape[0]
    head_size = inner // head_count

    for q in range(CHUNKS):
        locals_[q].wait()
        arrived = pl.ds(0, (col_count - 1) * width)
        pltpu.make_async_copy(
            rows_buf.at[pl.ds(q * chunk, chunk), arrived, :],
            rows_buf.at[pl.ds(q * chunk, chunk), arrived, :],
            norm_recv.at[q],
        ).wait()

        def body(i, carry):
            updated = row_update(
                own_ref[i],
                rows_buf[i],
                bias_buf,
                masking,
                wqg_ref[...],
                wkv_ref[...],
                gb_ref[...],
                ow_ref[...],
                ob_ref[...],
                head_count,
                head_size,
            )
            out_ref[i] = updated.astype(out_ref.dtype)
            return carry

        lax.fori_loop(q * chunk, (q + 1) * chunk, body, 0)

    for copy in norm_copies:
        copy.wait_send()
    for is_self, copy in bias_copies:

        @pl.when(jnp.logical_not(is_self))
        def _():
            copy.wait_send()


def fused(normed, payload, wqg, wkv, gate_bias, out_weight, out_bias):
    own_rows, width, channels = normed.shape
    cols = lax.axis_size("cols")
    rows = lax.axis_size("rows")
    slots, depth, _ = payload.shape
    group = rows // cols
    inner = out_weight.shape[0]
    vmem = pl.BlockSpec(memory_space=pltpu.VMEM)
    return pl.pallas_call(
        functools.partial(fused_kernel, slots - 1),
        out_shape=jax.ShapeDtypeStruct(normed.shape, jnp.bfloat16),
        in_specs=[vmem] * 7,
        out_specs=vmem,
        scratch_shapes=[
            pltpu.VMEM((own_rows, cols * width, channels), normed.dtype),
            pltpu.VMEM((rows,) + payload.shape, payload.dtype),
            pltpu.VMEM((slots, group * depth, cols * width), jnp.float32),
            pltpu.SemaphoreType.DMA((CHUNKS, cols)),
            pltpu.SemaphoreType.DMA((CHUNKS,)),
            pltpu.SemaphoreType.DMA((CHUNKS,)),
            pltpu.SemaphoreType.DMA((rows // 2,)),
            pltpu.SemaphoreType.DMA(()),
            pltpu.SemaphoreType.DMA((2,)),
        ],
        compiler_params=pltpu.CompilerParams(
            has_side_effects=True, collective_id=0, vmem_limit_bytes=48 * 1024 * 1024
        ),
    )(
        normed,
        payload,
        wqg,
        wkv,
        gate_bias.reshape(1, inner),
        out_weight,
        out_bias.reshape(1, channels),
    )


def shards(
    pair, token_mask, norm_gain, norm_shift, in_weight, gate_bias, bias_weight, out_weight, out_bias
):
    inner = out_weight.shape[0]
    normed = layer_norm(pair, norm_gain, norm_shift)
    bias_tile = jnp.einsum(
        "jkc,ch->hjk", normed, bias_weight, preferred_element_type=jnp.float32
    ).astype(jnp.bfloat16)
    mask_tile = jnp.broadcast_to(
        token_mask.astype(jnp.bfloat16)[None, None, :], (1,) + bias_tile.shape[1:]
    )
    payload = jnp.concatenate((bias_tile, mask_tile), axis=0)
    wqg = jnp.concatenate((in_weight[:, :inner], in_weight[:, 3 * inner :]), axis=1)
    wkv = in_weight[:, inner : 3 * inner]
    return fused(normed, payload, wqg, wkv, gate_bias, out_weight, out_bias)


def solution(mesh):
    placed = (P("rows", "cols", None), P("cols"), P(), P(), P(), P(), P(), P(), P())
    return jax.shard_map(
        shards, mesh=mesh, in_specs=placed, out_specs=P("rows", "cols", None), check_vma=False
    )
```

```python
import functools

import jax
import jax.numpy as jnp
from jax import lax
from jax.experimental import pallas as pl
from jax.experimental.pallas import tpu as pltpu
from jax.sharding import PartitionSpec as P


def layer_norm(pair_block, norm_gain, norm_shift):
    as_float = pair_block.astype(jnp.float32)
    center = jnp.mean(as_float, axis=-1, keepdims=True)
    spread = jnp.mean(jnp.square(as_float - center), axis=-1, keepdims=True)
    return ((as_float - center) * lax.rsqrt(spread + 1e-05) * norm_gain + norm_shift).astype(
        jnp.bfloat16
    )


CHUNKS = 4


def row_update(own, row, bias_ref, masking, wqg, wkv, gb, ow, ob, head_count, head_size):
    inner = head_count * head_size
    qg = jnp.dot(own, wqg, preferred_element_type=jnp.float32)
    queries = (qg[:, :inner] * head_size ** (-0.5)).astype(jnp.bfloat16)
    gates = jax.nn.sigmoid(qg[:, inner:] + gb)
    keys_t = lax.dot_general(
        wkv[:, :inner], row, (((0,), (1,)), ((), ())), preferred_element_type=jnp.float32
    ).astype(jnp.bfloat16)
    values = jnp.dot(row, wkv[:, inner:], preferred_element_type=jnp.float32).astype(jnp.bfloat16)
    lane_head = lax.broadcasted_iota(jnp.int32, (1, inner), 1) // head_size
    attended = jnp.zeros((own.shape[0], inner), jnp.float32)
    for h in range(head_count):
        in_head = lane_head == h
        q_h = jnp.where(in_head, queries, jnp.zeros_like(queries))
        scores = jnp.dot(q_h, keys_t, preferred_element_type=jnp.float32)
        scores = scores + bias_ref[h]
        scores = scores + masking
        top = jnp.max(scores, axis=-1, keepdims=True)
        expo = jnp.exp(scores - top)
        totals = jnp.sum(expo, axis=-1, keepdims=True)
        mixed = jnp.dot(expo.astype(jnp.bfloat16), values, preferred_element_type=jnp.float32)
        attended = jnp.where(in_head, mixed / totals, attended)
    gated = (gates * attended).astype(jnp.bfloat16)
    return jnp.dot(gated, ow, preferred_element_type=jnp.float32) + ob


def fused_kernel(
    head_count,
    own_ref,
    pay_ref,
    wqg_ref,
    wkv_ref,
    gb_ref,
    ow_ref,
    ob_ref,
    out_ref,
    rows_buf,
    pieces,
    bias_buf,
    norm_send,
    norm_recv,
    local_sem,
    bias_send,
    bias_recv,
    fwd_sem,
):
    col_count = lax.axis_size("cols")
    row_count = lax.axis_size("rows")
    group = row_count // col_count
    me_r = lax.axis_index("rows")
    me_c = lax.axis_index("cols")
    own_rows, width, channels = own_ref.shape
    depth = pay_ref.shape[0] - 1
    chunk = own_rows // CHUNKS
    mesh_id = pl.DeviceIdType.MESH
    target_c = me_r // group
    is_home = target_c == me_c
    parity = lax.rem(me_r, 2)
    half = row_count // 2
    sibling = me_r + 1 - 2 * parity
    barrier = pltpu.get_barrier_semaphore()
    for p in range(1, col_count):
        pl.semaphore_signal(
            barrier, 1, device_id=(me_r, lax.rem(me_c + p, col_count)), device_id_type=mesh_id
        )
    pl.semaphore_signal(barrier, 1, device_id=(sibling, me_c), device_id_type=mesh_id)
    for t in range(half):
        r = 2 * t + parity

        @pl.when(jnp.logical_not(jnp.logical_and(is_home, me_r == r)))
        def _():
            pl.semaphore_signal(barrier, 1, device_id=(r, target_c), device_id_type=mesh_id)

    for u in range(group // 2):
        for c in range(col_count):
            source = group * me_c + 2 * u + parity

            @pl.when(jnp.logical_not(jnp.logical_and(source == me_r, me_c == c)))
            def _():
                pl.semaphore_signal(barrier, 1, device_id=(source, c), device_id_type=mesh_id)

    pl.semaphore_wait(barrier, col_count + 2 * (half - is_home.astype(jnp.int32)))

    block = lax.rem(me_r, group)
    slot = lax.rem(block, 2) * half + (block // 2) * col_count + me_c
    local_bias = pltpu.make_async_copy(pay_ref, pieces.at[slot], bias_recv)
    bias_copies = []
    for t in range(half):
        r = 2 * t + parity
        is_self = jnp.logical_and(is_home, me_r == r)
        copy = pltpu.make_async_remote_copy(
            src_ref=pay_ref,
            dst_ref=pieces.at[slot],
            send_sem=bias_send.at[t],
            recv_sem=bias_recv,
            device_id=(r, target_c),
            device_id_type=mesh_id,
        )

        @pl.when(jnp.logical_not(is_self))
        def _():
            copy.start()

        @pl.when(is_self)
        def _():
            local_bias.start()

        bias_copies.append((is_self, copy))

    home = pl.ds(pl.multiple_of(me_c * width, width), width)
    norm_copies = []
    locals_ = []
    for q in range(CHUNKS):
        part = pl.ds(q * chunk, chunk)
        local = pltpu.make_async_copy(own_ref.at[part], rows_buf.at[part, home, :], local_sem.at[q])
        local.start()
        locals_.append(local)
        for p in range(1, col_count):
            copy = pltpu.make_async_remote_copy(
                src_ref=own_ref.at[part],
                dst_ref=rows_buf.at[part, home, :],
                send_sem=norm_send.at[q, p],
                recv_sem=norm_recv.at[q],
                device_id=(me_r, lax.rem(me_c + p, col_count)),
                device_id_type=mesh_id,
            )
            copy.start()
            norm_copies.append(copy)

    direct = pieces.at[pl.ds(pl.multiple_of(parity * half, half), half)]
    pltpu.make_async_copy(direct, direct, bias_recv).wait()
    forward = pltpu.make_async_remote_copy(
        src_ref=direct,
        dst_ref=direct,
        send_sem=fwd_sem.at[0],
        recv_sem=fwd_sem.at[1],
        device_id=(sibling, me_c),
        device_id_type=mesh_id,
    )
    forward.start()
    forward.wait()
    for c in range(col_count):
        for m in range(group):
            piece = pieces[(m % 2) * half + (m // 2) * col_count + c].astype(jnp.float32)
            for h in range(head_count):
                bias_buf[h, m * depth : (m + 1) * depth, c * width : (c + 1) * width] = piece[
                    :depth, h * width : (h + 1) * width
                ]
            if m == 0:
                bias_buf[head_count, 0:1, c * width : (c + 1) * width] = piece[
                    depth : depth + 1, 0:width
                ]
    masking = 1000000000.0 * (bias_buf[head_count, 0:1, :] - 1.0)
    inner = ow_ref.shape[0]
    head_size = inner // head_count

    for q in range(CHUNKS):
        locals_[q].wait()
        arrived = pl.ds(0, (col_count - 1) * width)
        pltpu.make_async_copy(
            rows_buf.at[pl.ds(q * chunk, chunk), arrived, :],
            rows_buf.at[pl.ds(q * chunk, chunk), arrived, :],
            norm_recv.at[q],
        ).wait()

        def body(i, carry):
            updated = row_update(
                own_ref[i],
                rows_buf[i],
                bias_buf,
                masking,
                wqg_ref[...],
                wkv_ref[...],
                gb_ref[...],
                ow_ref[...],
                ob_ref[...],
                head_count,
                head_size,
            )
            out_ref[i] = updated.astype(out_ref.dtype)
            return carry

        lax.fori_loop(q * chunk, (q + 1) * chunk, body, 0)

    for copy in norm_copies:
        copy.wait_send()
    for is_self, copy in bias_copies:

        @pl.when(jnp.logical_not(is_self))
        def _():
            copy.wait_send()


def fused(normed, payload, wqg, wkv, gate_bias, out_weight, out_bias, head_count):
    own_rows, width, channels = normed.shape
    cols = lax.axis_size("cols")
    rows = lax.axis_size("rows")
    slots = head_count + 1
    depth = payload.shape[0] - 1
    group = rows // cols
    inner = out_weight.shape[0]
    vmem = pl.BlockSpec(memory_space=pltpu.VMEM)
    return pl.pallas_call(
        functools.partial(fused_kernel, head_count),
        out_shape=jax.ShapeDtypeStruct(normed.shape, jnp.bfloat16),
        in_specs=[vmem] * 7,
        out_specs=vmem,
        scratch_shapes=[
            pltpu.VMEM((own_rows, cols * width, channels), normed.dtype),
            pltpu.VMEM((rows,) + payload.shape, payload.dtype),
            pltpu.VMEM((slots, group * depth, cols * width), jnp.float32),
            pltpu.SemaphoreType.DMA((CHUNKS, cols)),
            pltpu.SemaphoreType.DMA((CHUNKS,)),
            pltpu.SemaphoreType.DMA((CHUNKS,)),
            pltpu.SemaphoreType.DMA((rows // 2,)),
            pltpu.SemaphoreType.DMA(()),
            pltpu.SemaphoreType.DMA((2,)),
        ],
        compiler_params=pltpu.CompilerParams(
            has_side_effects=True, collective_id=0, vmem_limit_bytes=48 * 1024 * 1024
        ),
    )(
        normed,
        payload,
        wqg,
        wkv,
        gate_bias.reshape(1, inner),
        out_weight,
        out_bias.reshape(1, channels),
    )


def shards(
    pair, token_mask, norm_gain, norm_shift, in_weight, gate_bias, bias_weight, out_weight, out_bias
):
    inner = out_weight.shape[0]
    normed = layer_norm(pair, norm_gain, norm_shift)
    rows, width, _ = normed.shape
    head_count = bias_weight.shape[1]
    bias_tile = jnp.einsum(
        "jkc,ch->jhk", normed, bias_weight, preferred_element_type=jnp.float32
    ).astype(jnp.bfloat16)
    mask_row = jnp.tile(token_mask.astype(jnp.bfloat16), head_count)
    payload = jnp.concatenate(
        (bias_tile.reshape(rows, head_count * width), mask_row[None, :]), axis=0
    )
    wqg = jnp.concatenate((in_weight[:, :inner], in_weight[:, 3 * inner :]), axis=1)
    wkv = in_weight[:, inner : 3 * inner]
    return fused(normed, payload, wqg, wkv, gate_bias, out_weight, out_bias, head_count)


def solution(mesh):
    placed = (P("rows", "cols", None), P("cols"), P(), P(), P(), P(), P(), P(), P())
    return jax.shard_map(
        shards, mesh=mesh, in_specs=placed, out_specs=P("rows", "cols", None), check_vma=False
    )
```

```python
import functools

import jax
import jax.numpy as jnp
from jax import lax
from jax.experimental import pallas as pl
from jax.experimental.pallas import tpu as pltpu
from jax.sharding import PartitionSpec as P


def layer_norm(pair_block, norm_gain, norm_shift):
    as_float = pair_block.astype(jnp.float32)
    center = jnp.mean(as_float, axis=-1, keepdims=True)
    spread = jnp.mean(jnp.square(as_float - center), axis=-1, keepdims=True)
    return ((as_float - center) * lax.rsqrt(spread + 1e-05) * norm_gain + norm_shift).astype(
        jnp.bfloat16
    )


CHUNKS = 8


def row_update(own, row, bias_ref, masking, wqg, wkv, gb, ow, ob, head_count, head_size):
    inner = head_count * head_size
    qg = jnp.dot(own, wqg, preferred_element_type=jnp.float32)
    queries = (qg[:, :inner] * head_size ** (-0.5)).astype(jnp.bfloat16)
    gates = jax.nn.sigmoid(qg[:, inner:] + gb)
    keys_t = lax.dot_general(
        wkv[:, :inner], row, (((0,), (1,)), ((), ())), preferred_element_type=jnp.float32
    ).astype(jnp.bfloat16)
    values = jnp.dot(row, wkv[:, inner:], preferred_element_type=jnp.float32).astype(jnp.bfloat16)
    lane_head = lax.broadcasted_iota(jnp.int32, (1, inner), 1) // head_size
    attended = jnp.zeros((own.shape[0], inner), jnp.float32)
    for h in range(head_count):
        in_head = lane_head == h
        q_h = jnp.where(in_head, queries, jnp.zeros_like(queries))
        scores = jnp.dot(q_h, keys_t, preferred_element_type=jnp.float32)
        scores = scores + bias_ref[h]
        scores = scores + masking
        top = jnp.max(scores, axis=-1, keepdims=True)
        expo = jnp.exp(scores - top)
        totals = jnp.sum(expo, axis=-1, keepdims=True)
        mixed = jnp.dot(expo.astype(jnp.bfloat16), values, preferred_element_type=jnp.float32)
        attended = jnp.where(in_head, mixed / totals, attended)
    gated = (gates * attended).astype(jnp.bfloat16)
    return jnp.dot(gated, ow, preferred_element_type=jnp.float32) + ob


def fused_kernel(
    head_count,
    own_ref,
    pay_ref,
    wqg_ref,
    wkv_ref,
    gb_ref,
    ow_ref,
    ob_ref,
    out_ref,
    rows_buf,
    pieces,
    bias_buf,
    norm_send,
    norm_recv,
    local_sem,
    bias_send,
    bias_recv,
    fwd_sem,
):
    col_count = lax.axis_size("cols")
    row_count = lax.axis_size("rows")
    group = row_count // col_count
    me_r = lax.axis_index("rows")
    me_c = lax.axis_index("cols")
    own_rows, width, channels = own_ref.shape
    depth = pay_ref.shape[0] - 1
    chunk = own_rows // CHUNKS
    mesh_id = pl.DeviceIdType.MESH
    target_c = me_r // group
    is_home = target_c == me_c
    parity = lax.rem(me_r, 2)
    half = row_count // 2
    sibling = me_r + 1 - 2 * parity
    barrier = pltpu.get_barrier_semaphore()
    for p in range(1, col_count):
        pl.semaphore_signal(
            barrier, 1, device_id=(me_r, lax.rem(me_c + p, col_count)), device_id_type=mesh_id
        )
    pl.semaphore_signal(barrier, 1, device_id=(sibling, me_c), device_id_type=mesh_id)
    for t in range(half):
        r = 2 * t + parity

        @pl.when(jnp.logical_not(jnp.logical_and(is_home, me_r == r)))
        def _():
            pl.semaphore_signal(barrier, 1, device_id=(r, target_c), device_id_type=mesh_id)

    for u in range(group // 2):
        for c in range(col_count):
            source = group * me_c + 2 * u + parity

            @pl.when(jnp.logical_not(jnp.logical_and(source == me_r, me_c == c)))
            def _():
                pl.semaphore_signal(barrier, 1, device_id=(source, c), device_id_type=mesh_id)

    pl.semaphore_wait(barrier, col_count + 2 * (half - is_home.astype(jnp.int32)))

    block = lax.rem(me_r, group)
    slot = lax.rem(block, 2) * half + (block // 2) * col_count + me_c
    local_bias = pltpu.make_async_copy(pay_ref, pieces.at[slot], bias_recv)
    bias_copies = []
    for t in range(half):
        r = 2 * t + parity
        is_self = jnp.logical_and(is_home, me_r == r)
        copy = pltpu.make_async_remote_copy(
            src_ref=pay_ref,
            dst_ref=pieces.at[slot],
            send_sem=bias_send.at[t],
            recv_sem=bias_recv,
            device_id=(r, target_c),
            device_id_type=mesh_id,
        )

        @pl.when(jnp.logical_not(is_self))
        def _():
            copy.start()

        @pl.when(is_self)
        def _():
            local_bias.start()

        bias_copies.append((is_self, copy))

    home = pl.ds(pl.multiple_of(me_c * width, width), width)
    norm_copies = []
    locals_ = []
    for q in range(CHUNKS):
        part = pl.ds(q * chunk, chunk)
        local = pltpu.make_async_copy(own_ref.at[part], rows_buf.at[part, home, :], local_sem.at[q])
        local.start()
        locals_.append(local)
        for p in range(1, col_count):
            copy = pltpu.make_async_remote_copy(
                src_ref=own_ref.at[part],
                dst_ref=rows_buf.at[part, home, :],
                send_sem=norm_send.at[q, p],
                recv_sem=norm_recv.at[q],
                device_id=(me_r, lax.rem(me_c + p, col_count)),
                device_id_type=mesh_id,
            )
            copy.start()
            norm_copies.append(copy)

    direct = pieces.at[pl.ds(pl.multiple_of(parity * half, half), half)]
    pltpu.make_async_copy(direct, direct, bias_recv).wait()
    forward = pltpu.make_async_remote_copy(
        src_ref=direct,
        dst_ref=direct,
        send_sem=fwd_sem.at[0],
        recv_sem=fwd_sem.at[1],
        device_id=(sibling, me_c),
        device_id_type=mesh_id,
    )
    forward.start()
    forward.wait()
    for c in range(col_count):
        for m in range(group):
            piece = pieces[(m % 2) * half + (m // 2) * col_count + c].astype(jnp.float32)
            for h in range(head_count):
                bias_buf[h, m * depth : (m + 1) * depth, c * width : (c + 1) * width] = piece[
                    :depth, h * width : (h + 1) * width
                ]
            if m == 0:
                bias_buf[head_count, 0:1, c * width : (c + 1) * width] = piece[
                    depth : depth + 1, 0:width
                ]
    masking = 1000000000.0 * (bias_buf[head_count, 0:1, :] - 1.0)
    inner = ow_ref.shape[0]
    head_size = inner // head_count

    for q in range(CHUNKS):
        locals_[q].wait()
        arrived = pl.ds(0, (col_count - 1) * width)
        pltpu.make_async_copy(
            rows_buf.at[pl.ds(q * chunk, chunk), arrived, :],
            rows_buf.at[pl.ds(q * chunk, chunk), arrived, :],
            norm_recv.at[q],
        ).wait()

        def body(i, carry):
            updated = row_update(
                own_ref[i],
                rows_buf[i],
                bias_buf,
                masking,
                wqg_ref[...],
                wkv_ref[...],
                gb_ref[...],
                ow_ref[...],
                ob_ref[...],
                head_count,
                head_size,
            )
            out_ref[i] = updated.astype(out_ref.dtype)
            return carry

        lax.fori_loop(q * chunk, (q + 1) * chunk, body, 0)

    for copy in norm_copies:
        copy.wait_send()
    for is_self, copy in bias_copies:

        @pl.when(jnp.logical_not(is_self))
        def _():
            copy.wait_send()


def fused(normed, payload, wqg, wkv, gate_bias, out_weight, out_bias, head_count):
    own_rows, width, channels = normed.shape
    cols = lax.axis_size("cols")
    rows = lax.axis_size("rows")
    slots = head_count + 1
    depth = payload.shape[0] - 1
    group = rows // cols
    inner = out_weight.shape[0]
    vmem = pl.BlockSpec(memory_space=pltpu.VMEM)
    return pl.pallas_call(
        functools.partial(fused_kernel, head_count),
        out_shape=jax.ShapeDtypeStruct(normed.shape, jnp.bfloat16),
        in_specs=[vmem] * 7,
        out_specs=vmem,
        scratch_shapes=[
            pltpu.VMEM((own_rows, cols * width, channels), normed.dtype),
            pltpu.VMEM((rows,) + payload.shape, payload.dtype),
            pltpu.VMEM((slots, group * depth, cols * width), jnp.float32),
            pltpu.SemaphoreType.DMA((CHUNKS, cols)),
            pltpu.SemaphoreType.DMA((CHUNKS,)),
            pltpu.SemaphoreType.DMA((CHUNKS,)),
            pltpu.SemaphoreType.DMA((rows // 2,)),
            pltpu.SemaphoreType.DMA(()),
            pltpu.SemaphoreType.DMA((2,)),
        ],
        compiler_params=pltpu.CompilerParams(
            has_side_effects=True, collective_id=0, vmem_limit_bytes=48 * 1024 * 1024
        ),
    )(
        normed,
        payload,
        wqg,
        wkv,
        gate_bias.reshape(1, inner),
        out_weight,
        out_bias.reshape(1, channels),
    )


def shards(
    pair, token_mask, norm_gain, norm_shift, in_weight, gate_bias, bias_weight, out_weight, out_bias
):
    inner = out_weight.shape[0]
    normed = layer_norm(pair, norm_gain, norm_shift)
    rows, width, _ = normed.shape
    head_count = bias_weight.shape[1]
    bias_tile = jnp.einsum(
        "jkc,ch->jhk", normed, bias_weight, preferred_element_type=jnp.float32
    ).astype(jnp.bfloat16)
    mask_row = jnp.tile(token_mask.astype(jnp.bfloat16), head_count)
    payload = jnp.concatenate(
        (bias_tile.reshape(rows, head_count * width), mask_row[None, :]), axis=0
    )
    wqg = jnp.concatenate((in_weight[:, :inner], in_weight[:, 3 * inner :]), axis=1)
    wkv = in_weight[:, inner : 3 * inner]
    return fused(normed, payload, wqg, wkv, gate_bias, out_weight, out_bias, head_count)


def solution(mesh):
    placed = (P("rows", "cols", None), P("cols"), P(), P(), P(), P(), P(), P(), P())
    return jax.shard_map(
        shards, mesh=mesh, in_specs=placed, out_specs=P("rows", "cols", None), check_vma=False
    )
```

```python
import functools

import jax
import jax.numpy as jnp
from jax import lax
from jax.experimental import pallas as pl
from jax.experimental.pallas import tpu as pltpu
from jax.sharding import PartitionSpec as P


def layer_norm(pair_block, norm_gain, norm_shift):
    as_float = pair_block.astype(jnp.float32)
    center = jnp.mean(as_float, axis=-1, keepdims=True)
    spread = jnp.mean(jnp.square(as_float - center), axis=-1, keepdims=True)
    return ((as_float - center) * lax.rsqrt(spread + 1e-05) * norm_gain + norm_shift).astype(
        jnp.bfloat16
    )


CHUNKS = 8


def row_update(own, row, bias_ref, masking, wqg, wkv, gb, ow, ob, head_count, head_size):
    inner = head_count * head_size
    qg = jnp.dot(own, wqg, preferred_element_type=jnp.float32)
    queries = (qg[:, :inner] * head_size ** (-0.5)).astype(jnp.bfloat16)
    gates = jax.nn.sigmoid(qg[:, inner:] + gb)
    keys_t = lax.dot_general(
        wkv[:, :inner], row, (((0,), (1,)), ((), ())), preferred_element_type=jnp.float32
    ).astype(jnp.bfloat16)
    values = jnp.dot(row, wkv[:, inner:], preferred_element_type=jnp.float32).astype(jnp.bfloat16)
    lane_head = lax.broadcasted_iota(jnp.int32, (1, inner), 1) // head_size
    queries_rows = own.shape[0]
    stacked = jnp.concatenate(
        [jnp.where(lane_head == h, queries, jnp.zeros_like(queries)) for h in range(head_count)],
        axis=0,
    )
    scores = jnp.dot(stacked, keys_t, preferred_element_type=jnp.float32)
    scores = scores + bias_ref[0:head_count].reshape(head_count * queries_rows, -1)
    scores = scores + masking
    top = jnp.max(scores, axis=-1, keepdims=True)
    expo = jnp.exp(scores - top)
    totals = jnp.sum(expo, axis=-1, keepdims=True)
    mixed = jnp.dot(expo.astype(jnp.bfloat16), values, preferred_element_type=jnp.float32)
    attended = jnp.zeros((queries_rows, inner), jnp.float32)
    for h in range(head_count):
        rows_h = slice(h * queries_rows, (h + 1) * queries_rows)
        attended = jnp.where(lane_head == h, mixed[rows_h] / totals[rows_h], attended)
    gated = (gates * attended).astype(jnp.bfloat16)
    return jnp.dot(gated, ow, preferred_element_type=jnp.float32) + ob


def fused_kernel(
    head_count,
    own_ref,
    pay_ref,
    wqg_ref,
    wkv_ref,
    gb_ref,
    ow_ref,
    ob_ref,
    out_ref,
    rows_buf,
    pieces,
    bias_buf,
    norm_send,
    norm_recv,
    local_sem,
    bias_send,
    bias_recv,
    fwd_sem,
):
    col_count = lax.axis_size("cols")
    row_count = lax.axis_size("rows")
    group = row_count // col_count
    me_r = lax.axis_index("rows")
    me_c = lax.axis_index("cols")
    own_rows, width, channels = own_ref.shape
    depth = pay_ref.shape[0] - 1
    chunk = own_rows // CHUNKS
    mesh_id = pl.DeviceIdType.MESH
    target_c = me_r // group
    is_home = target_c == me_c
    parity = lax.rem(me_r, 2)
    half = row_count // 2
    sibling = me_r + 1 - 2 * parity
    barrier = pltpu.get_barrier_semaphore()
    for p in range(1, col_count):
        pl.semaphore_signal(
            barrier, 1, device_id=(me_r, lax.rem(me_c + p, col_count)), device_id_type=mesh_id
        )
    pl.semaphore_signal(barrier, 1, device_id=(sibling, me_c), device_id_type=mesh_id)
    for t in range(half):
        r = 2 * t + parity

        @pl.when(jnp.logical_not(jnp.logical_and(is_home, me_r == r)))
        def _():
            pl.semaphore_signal(barrier, 1, device_id=(r, target_c), device_id_type=mesh_id)

    for u in range(group // 2):
        for c in range(col_count):
            source = group * me_c + 2 * u + parity

            @pl.when(jnp.logical_not(jnp.logical_and(source == me_r, me_c == c)))
            def _():
                pl.semaphore_signal(barrier, 1, device_id=(source, c), device_id_type=mesh_id)

    pl.semaphore_wait(barrier, col_count + 2 * (half - is_home.astype(jnp.int32)))

    block = lax.rem(me_r, group)
    slot = lax.rem(block, 2) * half + (block // 2) * col_count + me_c
    local_bias = pltpu.make_async_copy(pay_ref, pieces.at[slot], bias_recv)
    bias_copies = []
    for t in range(half):
        r = 2 * t + parity
        is_self = jnp.logical_and(is_home, me_r == r)
        copy = pltpu.make_async_remote_copy(
            src_ref=pay_ref,
            dst_ref=pieces.at[slot],
            send_sem=bias_send.at[t],
            recv_sem=bias_recv,
            device_id=(r, target_c),
            device_id_type=mesh_id,
        )

        @pl.when(jnp.logical_not(is_self))
        def _():
            copy.start()

        @pl.when(is_self)
        def _():
            local_bias.start()

        bias_copies.append((is_self, copy))

    home = pl.ds(pl.multiple_of(me_c * width, width), width)
    norm_copies = []
    locals_ = []
    for q in range(CHUNKS):
        part = pl.ds(q * chunk, chunk)
        local = pltpu.make_async_copy(own_ref.at[part], rows_buf.at[part, home, :], local_sem.at[q])
        local.start()
        locals_.append(local)
        for p in range(1, col_count):
            copy = pltpu.make_async_remote_copy(
                src_ref=own_ref.at[part],
                dst_ref=rows_buf.at[part, home, :],
                send_sem=norm_send.at[q, p],
                recv_sem=norm_recv.at[q],
                device_id=(me_r, lax.rem(me_c + p, col_count)),
                device_id_type=mesh_id,
            )
            copy.start()
            norm_copies.append(copy)

    direct = pieces.at[pl.ds(pl.multiple_of(parity * half, half), half)]
    pltpu.make_async_copy(direct, direct, bias_recv).wait()
    forward = pltpu.make_async_remote_copy(
        src_ref=direct,
        dst_ref=direct,
        send_sem=fwd_sem.at[0],
        recv_sem=fwd_sem.at[1],
        device_id=(sibling, me_c),
        device_id_type=mesh_id,
    )
    forward.start()
    forward.wait()
    for c in range(col_count):
        for m in range(group):
            piece = pieces[(m % 2) * half + (m // 2) * col_count + c].astype(jnp.float32)
            for h in range(head_count):
                bias_buf[h, m * depth : (m + 1) * depth, c * width : (c + 1) * width] = piece[
                    :depth, h * width : (h + 1) * width
                ]
            if m == 0:
                bias_buf[head_count, 0:1, c * width : (c + 1) * width] = piece[
                    depth : depth + 1, 0:width
                ]
    masking = 1000000000.0 * (bias_buf[head_count, 0:1, :] - 1.0)
    inner = ow_ref.shape[0]
    head_size = inner // head_count

    for q in range(CHUNKS):
        locals_[q].wait()
        arrived = pl.ds(0, (col_count - 1) * width)
        pltpu.make_async_copy(
            rows_buf.at[pl.ds(q * chunk, chunk), arrived, :],
            rows_buf.at[pl.ds(q * chunk, chunk), arrived, :],
            norm_recv.at[q],
        ).wait()

        def body(i, carry):
            updated = row_update(
                own_ref[i],
                rows_buf[i],
                bias_buf,
                masking,
                wqg_ref[...],
                wkv_ref[...],
                gb_ref[...],
                ow_ref[...],
                ob_ref[...],
                head_count,
                head_size,
            )
            out_ref[i] = updated.astype(out_ref.dtype)
            return carry

        lax.fori_loop(q * chunk, (q + 1) * chunk, body, 0)

    for copy in norm_copies:
        copy.wait_send()
    for is_self, copy in bias_copies:

        @pl.when(jnp.logical_not(is_self))
        def _():
            copy.wait_send()


def fused(normed, payload, wqg, wkv, gate_bias, out_weight, out_bias, head_count):
    own_rows, width, channels = normed.shape
    cols = lax.axis_size("cols")
    rows = lax.axis_size("rows")
    slots = head_count + 1
    depth = payload.shape[0] - 1
    group = rows // cols
    inner = out_weight.shape[0]
    vmem = pl.BlockSpec(memory_space=pltpu.VMEM)
    return pl.pallas_call(
        functools.partial(fused_kernel, head_count),
        out_shape=jax.ShapeDtypeStruct(normed.shape, jnp.bfloat16),
        in_specs=[vmem] * 7,
        out_specs=vmem,
        scratch_shapes=[
            pltpu.VMEM((own_rows, cols * width, channels), normed.dtype),
            pltpu.VMEM((rows,) + payload.shape, payload.dtype),
            pltpu.VMEM((slots, group * depth, cols * width), jnp.float32),
            pltpu.SemaphoreType.DMA((CHUNKS, cols)),
            pltpu.SemaphoreType.DMA((CHUNKS,)),
            pltpu.SemaphoreType.DMA((CHUNKS,)),
            pltpu.SemaphoreType.DMA((rows // 2,)),
            pltpu.SemaphoreType.DMA(()),
            pltpu.SemaphoreType.DMA((2,)),
        ],
        compiler_params=pltpu.CompilerParams(
            has_side_effects=True, collective_id=0, vmem_limit_bytes=48 * 1024 * 1024
        ),
    )(
        normed,
        payload,
        wqg,
        wkv,
        gate_bias.reshape(1, inner),
        out_weight,
        out_bias.reshape(1, channels),
    )


def shards(
    pair, token_mask, norm_gain, norm_shift, in_weight, gate_bias, bias_weight, out_weight, out_bias
):
    inner = out_weight.shape[0]
    normed = layer_norm(pair, norm_gain, norm_shift)
    rows, width, _ = normed.shape
    head_count = bias_weight.shape[1]
    bias_tile = jnp.einsum(
        "jkc,ch->jhk", normed, bias_weight, preferred_element_type=jnp.float32
    ).astype(jnp.bfloat16)
    mask_row = jnp.tile(token_mask.astype(jnp.bfloat16), head_count)
    payload = jnp.concatenate(
        (bias_tile.reshape(rows, head_count * width), mask_row[None, :]), axis=0
    )
    wqg = jnp.concatenate((in_weight[:, :inner], in_weight[:, 3 * inner :]), axis=1)
    wkv = in_weight[:, inner : 3 * inner]
    return fused(normed, payload, wqg, wkv, gate_bias, out_weight, out_bias, head_count)


def solution(mesh):
    placed = (P("rows", "cols", None), P("cols"), P(), P(), P(), P(), P(), P(), P())
    return jax.shard_map(
        shards, mesh=mesh, in_specs=placed, out_specs=P("rows", "cols", None), check_vma=False
    )
```

```python
import functools

import jax
import jax.numpy as jnp
from jax import lax
from jax.experimental import pallas as pl
from jax.experimental.pallas import tpu as pltpu
from jax.sharding import PartitionSpec as P


def layer_norm(pair_block, norm_gain, norm_shift):
    as_float = pair_block.astype(jnp.float32)
    center = jnp.mean(as_float, axis=-1, keepdims=True)
    spread = jnp.mean(jnp.square(as_float - center), axis=-1, keepdims=True)
    return ((as_float - center) * lax.rsqrt(spread + 1e-05) * norm_gain + norm_shift).astype(
        jnp.bfloat16
    )


CHUNKS = 8


def row_update(own, row, bias_ref, masking, wqg, wkv, gb, ow, ob, head_count, head_size):
    inner = head_count * head_size
    qg = jnp.dot(own, wqg, preferred_element_type=jnp.float32)
    queries = (qg[:, :inner] * head_size ** (-0.5)).astype(jnp.bfloat16)
    gates = jax.nn.sigmoid(qg[:, inner:] + gb)
    keys_t = lax.dot_general(
        wkv[:, :inner], row, (((0,), (1,)), ((), ())), preferred_element_type=jnp.float32
    ).astype(jnp.bfloat16)
    values = jnp.dot(row, wkv[:, inner:], preferred_element_type=jnp.float32).astype(jnp.bfloat16)
    lane_head = lax.broadcasted_iota(jnp.int32, (1, inner), 1) // head_size
    queries_rows = own.shape[0]
    stacked = jnp.concatenate(
        [jnp.where(lane_head == h, queries, jnp.zeros_like(queries)) for h in range(head_count)],
        axis=0,
    )
    scores = jnp.dot(stacked, keys_t, preferred_element_type=jnp.float32)
    scores = scores + bias_ref[0:head_count].reshape(head_count * queries_rows, -1)
    scores = scores + masking
    top = jnp.max(scores, axis=-1, keepdims=True)
    expo = jnp.exp(scores - top)
    totals = jnp.sum(expo, axis=-1, keepdims=True)
    mixed = jnp.dot(expo.astype(jnp.bfloat16), values, preferred_element_type=jnp.float32)
    attended = jnp.zeros((queries_rows, inner), jnp.float32)
    for h in range(head_count):
        rows_h = slice(h * queries_rows, (h + 1) * queries_rows)
        attended = jnp.where(lane_head == h, mixed[rows_h] / totals[rows_h], attended)
    gated = (gates * attended).astype(jnp.bfloat16)
    return jnp.dot(gated, ow, preferred_element_type=jnp.float32) + ob


def fused_kernel(
    head_count,
    own_ref,
    pay_ref,
    wqg_ref,
    wkv_ref,
    gb_ref,
    ow_ref,
    ob_ref,
    out_ref,
    rows_buf,
    pieces,
    bias_buf,
    norm_send,
    norm_recv,
    local_sem,
    bias_send,
    bias_recv,
    fwd_sem,
):
    col_count = lax.axis_size("cols")
    row_count = lax.axis_size("rows")
    group = row_count // col_count
    me_r = lax.axis_index("rows")
    me_c = lax.axis_index("cols")
    own_rows, width, channels = own_ref.shape
    depth = pay_ref.shape[0] - 1
    chunk = own_rows // CHUNKS
    mesh_id = pl.DeviceIdType.MESH
    target_c = me_r // group
    is_home = target_c == me_c
    parity = lax.rem(me_r, 2)
    half = row_count // 2
    sibling = me_r + 1 - 2 * parity
    barrier = pltpu.get_barrier_semaphore()
    for p in range(1, col_count):
        pl.semaphore_signal(
            barrier, 1, device_id=(me_r, lax.rem(me_c + p, col_count)), device_id_type=mesh_id
        )
    pl.semaphore_signal(barrier, 1, device_id=(sibling, me_c), device_id_type=mesh_id)
    for t in range(half):
        r = 2 * t + parity

        @pl.when(jnp.logical_not(jnp.logical_and(is_home, me_r == r)))
        def _():
            pl.semaphore_signal(barrier, 1, device_id=(r, target_c), device_id_type=mesh_id)

    for u in range(group // 2):
        for c in range(col_count):
            source = group * me_c + 2 * u + parity

            @pl.when(jnp.logical_not(jnp.logical_and(source == me_r, me_c == c)))
            def _():
                pl.semaphore_signal(barrier, 1, device_id=(source, c), device_id_type=mesh_id)

    pl.semaphore_wait(barrier, col_count + 2 * (half - is_home.astype(jnp.int32)))

    block = lax.rem(me_r, group)
    slot = lax.rem(block, 2) * half + (block // 2) * col_count + me_c
    local_bias = pltpu.make_async_copy(pay_ref, pieces.at[slot], bias_recv)
    bias_copies = []
    for t in range(half):
        r = 2 * t + parity
        is_self = jnp.logical_and(is_home, me_r == r)
        copy = pltpu.make_async_remote_copy(
            src_ref=pay_ref,
            dst_ref=pieces.at[slot],
            send_sem=bias_send.at[t],
            recv_sem=bias_recv,
            device_id=(r, target_c),
            device_id_type=mesh_id,
        )

        @pl.when(jnp.logical_not(is_self))
        def _():
            copy.start()

        @pl.when(is_self)
        def _():
            local_bias.start()

        bias_copies.append((is_self, copy))

    home = pl.ds(pl.multiple_of(me_c * width, width), width)
    norm_copies = []
    locals_ = []
    for q in range(CHUNKS):
        part = pl.ds(q * chunk, chunk)
        local = pltpu.make_async_copy(own_ref.at[part], rows_buf.at[part, home, :], local_sem.at[q])
        local.start()
        locals_.append(local)
        for p in range(1, col_count):
            copy = pltpu.make_async_remote_copy(
                src_ref=own_ref.at[part],
                dst_ref=rows_buf.at[part, home, :],
                send_sem=norm_send.at[q, p],
                recv_sem=norm_recv.at[q],
                device_id=(me_r, lax.rem(me_c + p, col_count)),
                device_id_type=mesh_id,
            )
            copy.start()
            norm_copies.append(copy)

    direct = pieces.at[pl.ds(pl.multiple_of(parity * half, half), half)]
    pltpu.make_async_copy(direct, direct, bias_recv).wait()
    forward = pltpu.make_async_remote_copy(
        src_ref=direct,
        dst_ref=direct,
        send_sem=fwd_sem.at[0],
        recv_sem=fwd_sem.at[1],
        device_id=(sibling, me_c),
        device_id_type=mesh_id,
    )
    forward.start()
    forward.wait()
    for c in range(col_count):
        for m in range(group):
            piece = pieces[(m % 2) * half + (m // 2) * col_count + c].astype(jnp.float32)
            for h in range(head_count):
                bias_buf[h, m * depth : (m + 1) * depth, c * width : (c + 1) * width] = piece[
                    :depth, h * width : (h + 1) * width
                ]
            if m == 0:
                bias_buf[head_count, 0:1, c * width : (c + 1) * width] = piece[
                    depth : depth + 1, 0:width
                ]
    masking = 1000000000.0 * (bias_buf[head_count, 0:1, :] - 1.0)
    inner = ow_ref.shape[0]
    head_size = inner // head_count

    for q in range(CHUNKS):
        locals_[q].wait()
        arrived = pl.ds(0, (col_count - 1) * width)
        pltpu.make_async_copy(
            rows_buf.at[pl.ds(q * chunk, chunk), arrived, :],
            rows_buf.at[pl.ds(q * chunk, chunk), arrived, :],
            norm_recv.at[q],
        ).wait()

        def body(i, carry):
            updated = row_update(
                own_ref[i],
                rows_buf[i],
                bias_buf,
                masking,
                wqg_ref[...],
                wkv_ref[...],
                gb_ref[...],
                ow_ref[...],
                ob_ref[...],
                head_count,
                head_size,
            )
            out_ref[i] = updated.astype(out_ref.dtype)
            return carry

        lax.fori_loop(q * chunk, (q + 1) * chunk, body, 0, unroll=True)

    for copy in norm_copies:
        copy.wait_send()
    for is_self, copy in bias_copies:

        @pl.when(jnp.logical_not(is_self))
        def _():
            copy.wait_send()


def fused(normed, payload, wqg, wkv, gate_bias, out_weight, out_bias, head_count):
    own_rows, width, channels = normed.shape
    cols = lax.axis_size("cols")
    rows = lax.axis_size("rows")
    slots = head_count + 1
    depth = payload.shape[0] - 1
    group = rows // cols
    inner = out_weight.shape[0]
    vmem = pl.BlockSpec(memory_space=pltpu.VMEM)
    return pl.pallas_call(
        functools.partial(fused_kernel, head_count),
        out_shape=jax.ShapeDtypeStruct(normed.shape, jnp.bfloat16),
        in_specs=[vmem] * 7,
        out_specs=vmem,
        scratch_shapes=[
            pltpu.VMEM((own_rows, cols * width, channels), normed.dtype),
            pltpu.VMEM((rows,) + payload.shape, payload.dtype),
            pltpu.VMEM((slots, group * depth, cols * width), jnp.float32),
            pltpu.SemaphoreType.DMA((CHUNKS, cols)),
            pltpu.SemaphoreType.DMA((CHUNKS,)),
            pltpu.SemaphoreType.DMA((CHUNKS,)),
            pltpu.SemaphoreType.DMA((rows // 2,)),
            pltpu.SemaphoreType.DMA(()),
            pltpu.SemaphoreType.DMA((2,)),
        ],
        compiler_params=pltpu.CompilerParams(
            has_side_effects=True, collective_id=0, vmem_limit_bytes=48 * 1024 * 1024
        ),
    )(
        normed,
        payload,
        wqg,
        wkv,
        gate_bias.reshape(1, inner),
        out_weight,
        out_bias.reshape(1, channels),
    )


def shards(
    pair, token_mask, norm_gain, norm_shift, in_weight, gate_bias, bias_weight, out_weight, out_bias
):
    inner = out_weight.shape[0]
    normed = layer_norm(pair, norm_gain, norm_shift)
    rows, width, _ = normed.shape
    head_count = bias_weight.shape[1]
    bias_tile = jnp.einsum(
        "jkc,ch->jhk", normed, bias_weight, preferred_element_type=jnp.float32
    ).astype(jnp.bfloat16)
    mask_row = jnp.tile(token_mask.astype(jnp.bfloat16), head_count)
    payload = jnp.concatenate(
        (bias_tile.reshape(rows, head_count * width), mask_row[None, :]), axis=0
    )
    wqg = jnp.concatenate((in_weight[:, :inner], in_weight[:, 3 * inner :]), axis=1)
    wkv = in_weight[:, inner : 3 * inner]
    return fused(normed, payload, wqg, wkv, gate_bias, out_weight, out_bias, head_count)


def solution(mesh):
    placed = (P("rows", "cols", None), P("cols"), P(), P(), P(), P(), P(), P(), P())
    return jax.shard_map(
        shards, mesh=mesh, in_specs=placed, out_specs=P("rows", "cols", None), check_vma=False
    )
```

```python
import functools

import jax
import jax.numpy as jnp
from jax import lax
from jax.experimental import pallas as pl
from jax.experimental.pallas import tpu as pltpu
from jax.sharding import PartitionSpec as P


CHUNKS = 8


def row_update(own, row, bias_ref, masking, wqg, wkv, gb, ow, ob, head_count, head_size):
    inner = head_count * head_size
    qg = jnp.dot(own, wqg, preferred_element_type=jnp.float32)
    queries = (qg[:, :inner] * head_size ** (-0.5)).astype(jnp.bfloat16)
    gates = jax.nn.sigmoid(qg[:, inner:] + gb)
    keys_t = lax.dot_general(
        wkv[:, :inner], row, (((0,), (1,)), ((), ())), preferred_element_type=jnp.float32
    ).astype(jnp.bfloat16)
    values = jnp.dot(row, wkv[:, inner:], preferred_element_type=jnp.float32).astype(jnp.bfloat16)
    lane_head = lax.broadcasted_iota(jnp.int32, (1, inner), 1) // head_size
    queries_rows = own.shape[0]
    stacked = jnp.concatenate(
        [jnp.where(lane_head == h, queries, jnp.zeros_like(queries)) for h in range(head_count)],
        axis=0,
    )
    scores = jnp.dot(stacked, keys_t, preferred_element_type=jnp.float32)
    scores = scores + bias_ref[0:head_count].reshape(head_count * queries_rows, -1)
    scores = scores + masking
    top = jnp.max(scores, axis=-1, keepdims=True)
    expo = jnp.exp(scores - top)
    totals = jnp.sum(expo, axis=-1, keepdims=True)
    mixed = jnp.dot(expo.astype(jnp.bfloat16), values, preferred_element_type=jnp.float32)
    attended = jnp.zeros((queries_rows, inner), jnp.float32)
    for h in range(head_count):
        rows_h = slice(h * queries_rows, (h + 1) * queries_rows)
        attended = jnp.where(lane_head == h, mixed[rows_h] / totals[rows_h], attended)
    gated = (gates * attended).astype(jnp.bfloat16)
    return jnp.dot(gated, ow, preferred_element_type=jnp.float32) + ob


def fused_kernel(
    head_count,
    pair_ref,
    mask_ref,
    gain_ref,
    shift_ref,
    bwt_ref,
    wqg_ref,
    wkv_ref,
    gb_ref,
    ow_ref,
    ob_ref,
    out_ref,
    own_ref,
    pay_ref,
    rows_buf,
    pieces,
    bias_buf,
    norm_send,
    norm_recv,
    local_sem,
    bias_send,
    bias_recv,
    fwd_sem,
):
    col_count = lax.axis_size("cols")
    row_count = lax.axis_size("rows")
    group = row_count // col_count
    me_r = lax.axis_index("rows")
    me_c = lax.axis_index("cols")
    own_rows, width, channels = pair_ref.shape
    depth = own_rows
    chunk = own_rows // CHUNKS
    mesh_id = pl.DeviceIdType.MESH
    target_c = me_r // group
    is_home = target_c == me_c
    parity = lax.rem(me_r, 2)
    half = row_count // 2
    sibling = me_r + 1 - 2 * parity
    barrier = pltpu.get_barrier_semaphore()
    for p in range(1, col_count):
        pl.semaphore_signal(
            barrier, 1, device_id=(me_r, lax.rem(me_c + p, col_count)), device_id_type=mesh_id
        )
    pl.semaphore_signal(barrier, 1, device_id=(sibling, me_c), device_id_type=mesh_id)
    for t in range(half):
        r = 2 * t + parity

        @pl.when(jnp.logical_not(jnp.logical_and(is_home, me_r == r)))
        def _():
            pl.semaphore_signal(barrier, 1, device_id=(r, target_c), device_id_type=mesh_id)

    for u in range(group // 2):
        for c in range(col_count):
            source = group * me_c + 2 * u + parity

            @pl.when(jnp.logical_not(jnp.logical_and(source == me_r, me_c == c)))
            def _():
                pl.semaphore_signal(barrier, 1, device_id=(source, c), device_id_type=mesh_id)

    as_float = pair_ref[...].astype(jnp.float32)
    center = jnp.mean(as_float, axis=-1, keepdims=True)
    spread = jnp.mean(jnp.square(as_float - center), axis=-1, keepdims=True)
    normed = (
        (as_float - center) * lax.rsqrt(spread + 1e-05) * gain_ref[...] + shift_ref[...]
    ).astype(jnp.bfloat16)
    own_ref[...] = normed
    flat = normed.reshape(own_rows * width, channels)
    bias_t = lax.dot_general(
        bwt_ref[...], flat, (((1,), (1,)), ((), ())), preferred_element_type=jnp.float32
    ).astype(jnp.bfloat16)
    mask_row = mask_ref[...].astype(jnp.float32).astype(jnp.bfloat16)
    for h in range(head_count):
        for j in range(own_rows):
            pay_ref[j : j + 1, h * width : (h + 1) * width] = bias_t[
                h : h + 1, j * width : (j + 1) * width
            ]
        pay_ref[own_rows : own_rows + 1, h * width : (h + 1) * width] = mask_row

    pl.semaphore_wait(barrier, col_count + 2 * (half - is_home.astype(jnp.int32)))

    block = lax.rem(me_r, group)
    slot = lax.rem(block, 2) * half + (block // 2) * col_count + me_c
    local_bias = pltpu.make_async_copy(pay_ref, pieces.at[slot], bias_recv)
    bias_copies = []
    for t in range(half):
        r = 2 * t + parity
        is_self = jnp.logical_and(is_home, me_r == r)
        copy = pltpu.make_async_remote_copy(
            src_ref=pay_ref,
            dst_ref=pieces.at[slot],
            send_sem=bias_send.at[t],
            recv_sem=bias_recv,
            device_id=(r, target_c),
            device_id_type=mesh_id,
        )

        @pl.when(jnp.logical_not(is_self))
        def _():
            copy.start()

        @pl.when(is_self)
        def _():
            local_bias.start()

        bias_copies.append((is_self, copy))

    home = pl.ds(pl.multiple_of(me_c * width, width), width)
    norm_copies = []
    locals_ = []
    for q in range(CHUNKS):
        part = pl.ds(q * chunk, chunk)
        local = pltpu.make_async_copy(own_ref.at[part], rows_buf.at[part, home, :], local_sem.at[q])
        local.start()
        locals_.append(local)
        for p in range(1, col_count):
            copy = pltpu.make_async_remote_copy(
                src_ref=own_ref.at[part],
                dst_ref=rows_buf.at[part, home, :],
                send_sem=norm_send.at[q, p],
                recv_sem=norm_recv.at[q],
                device_id=(me_r, lax.rem(me_c + p, col_count)),
                device_id_type=mesh_id,
            )
            copy.start()
            norm_copies.append(copy)

    direct = pieces.at[pl.ds(pl.multiple_of(parity * half, half), half)]
    pltpu.make_async_copy(direct, direct, bias_recv).wait()
    forward = pltpu.make_async_remote_copy(
        src_ref=direct,
        dst_ref=direct,
        send_sem=fwd_sem.at[0],
        recv_sem=fwd_sem.at[1],
        device_id=(sibling, me_c),
        device_id_type=mesh_id,
    )
    forward.start()
    forward.wait()
    for c in range(col_count):
        for m in range(group):
            piece = pieces[(m % 2) * half + (m // 2) * col_count + c].astype(jnp.float32)
            for h in range(head_count):
                bias_buf[h, m * depth : (m + 1) * depth, c * width : (c + 1) * width] = piece[
                    :depth, h * width : (h + 1) * width
                ]
            if m == 0:
                bias_buf[head_count, 0:1, c * width : (c + 1) * width] = piece[
                    depth : depth + 1, 0:width
                ]
    masking = 1000000000.0 * (bias_buf[head_count, 0:1, :] - 1.0)
    inner = ow_ref.shape[0]
    head_size = inner // head_count

    for q in range(CHUNKS):
        locals_[q].wait()
        arrived = pl.ds(0, (col_count - 1) * width)
        pltpu.make_async_copy(
            rows_buf.at[pl.ds(q * chunk, chunk), arrived, :],
            rows_buf.at[pl.ds(q * chunk, chunk), arrived, :],
            norm_recv.at[q],
        ).wait()

        def body(i, carry):
            updated = row_update(
                own_ref[i],
                rows_buf[i],
                bias_buf,
                masking,
                wqg_ref[...],
                wkv_ref[...],
                gb_ref[...],
                ow_ref[...],
                ob_ref[...],
                head_count,
                head_size,
            )
            out_ref[i] = updated.astype(out_ref.dtype)
            return carry

        lax.fori_loop(q * chunk, (q + 1) * chunk, body, 0)

    for copy in norm_copies:
        copy.wait_send()
    for is_self, copy in bias_copies:

        @pl.when(jnp.logical_not(is_self))
        def _():
            copy.wait_send()


def fused(pair, token_mask, norm_gain, norm_shift, bias_weight, wqg, wkv, gate_bias, out_weight, out_bias):
    own_rows, width, channels = pair.shape
    cols = lax.axis_size("cols")
    rows = lax.axis_size("rows")
    head_count = bias_weight.shape[1]
    slots = head_count + 1
    depth = own_rows
    group = rows // cols
    inner = out_weight.shape[0]
    vmem = pl.BlockSpec(memory_space=pltpu.VMEM)
    payload_shape = (own_rows + 1, head_count * width)
    return pl.pallas_call(
        functools.partial(fused_kernel, head_count),
        out_shape=jax.ShapeDtypeStruct(pair.shape, jnp.bfloat16),
        in_specs=[vmem] * 10,
        out_specs=vmem,
        scratch_shapes=[
            pltpu.VMEM(pair.shape, jnp.bfloat16),
            pltpu.VMEM(payload_shape, jnp.bfloat16),
            pltpu.VMEM((own_rows, cols * width, channels), jnp.bfloat16),
            pltpu.VMEM((rows,) + payload_shape, jnp.bfloat16),
            pltpu.VMEM((slots, group * depth, cols * width), jnp.float32),
            pltpu.SemaphoreType.DMA((CHUNKS, cols)),
            pltpu.SemaphoreType.DMA((CHUNKS,)),
            pltpu.SemaphoreType.DMA((CHUNKS,)),
            pltpu.SemaphoreType.DMA((rows // 2,)),
            pltpu.SemaphoreType.DMA(()),
            pltpu.SemaphoreType.DMA((2,)),
        ],
        compiler_params=pltpu.CompilerParams(
            has_side_effects=True, collective_id=0, vmem_limit_bytes=48 * 1024 * 1024
        ),
    )(
        pair,
        token_mask.reshape(1, width),
        norm_gain.reshape(1, channels),
        norm_shift.reshape(1, channels),
        bias_weight.T,
        wqg,
        wkv,
        gate_bias.reshape(1, inner),
        out_weight,
        out_bias.reshape(1, channels),
    )


def shards(
    pair, token_mask, norm_gain, norm_shift, in_weight, gate_bias, bias_weight, out_weight, out_bias
):
    inner = out_weight.shape[0]
    wqg = jnp.concatenate((in_weight[:, :inner], in_weight[:, 3 * inner :]), axis=1)
    wkv = in_weight[:, inner : 3 * inner]
    return fused(
        pair, token_mask, norm_gain, norm_shift, bias_weight, wqg, wkv, gate_bias, out_weight, out_bias
    )


def solution(mesh):
    placed = (P("rows", "cols", None), P("cols"), P(), P(), P(), P(), P(), P(), P())
    return jax.shard_map(
        shards, mesh=mesh, in_specs=placed, out_specs=P("rows", "cols", None), check_vma=False
    )
```

```python
import functools

import jax
import jax.numpy as jnp
from jax import lax
from jax.experimental import pallas as pl
from jax.experimental.pallas import tpu as pltpu
from jax.sharding import PartitionSpec as P


CHUNKS = 12


def row_update(own, row, bias_ref, masking, wqg, wkv, gb, ow, ob, head_count, head_size):
    inner = head_count * head_size
    qg = jnp.dot(own, wqg, preferred_element_type=jnp.float32)
    queries = (qg[:, :inner] * head_size ** (-0.5)).astype(jnp.bfloat16)
    gates = jax.nn.sigmoid(qg[:, inner:] + gb)
    keys_t = lax.dot_general(
        wkv[:, :inner], row, (((0,), (1,)), ((), ())), preferred_element_type=jnp.float32
    ).astype(jnp.bfloat16)
    values = jnp.dot(row, wkv[:, inner:], preferred_element_type=jnp.float32).astype(jnp.bfloat16)
    lane_head = lax.broadcasted_iota(jnp.int32, (1, inner), 1) // head_size
    queries_rows = own.shape[0]
    stacked = jnp.concatenate(
        [jnp.where(lane_head == h, queries, jnp.zeros_like(queries)) for h in range(head_count)],
        axis=0,
    )
    scores = jnp.dot(stacked, keys_t, preferred_element_type=jnp.float32)
    scores = scores + bias_ref[0:head_count].reshape(head_count * queries_rows, -1)
    scores = scores + masking
    top = jnp.max(scores, axis=-1, keepdims=True)
    expo = jnp.exp(scores - top)
    totals = jnp.sum(expo, axis=-1, keepdims=True)
    mixed = jnp.dot(expo.astype(jnp.bfloat16), values, preferred_element_type=jnp.float32)
    attended = jnp.zeros((queries_rows, inner), jnp.float32)
    for h in range(head_count):
        rows_h = slice(h * queries_rows, (h + 1) * queries_rows)
        attended = jnp.where(lane_head == h, mixed[rows_h] / totals[rows_h], attended)
    gated = (gates * attended).astype(jnp.bfloat16)
    return jnp.dot(gated, ow, preferred_element_type=jnp.float32) + ob


def fused_kernel(
    head_count,
    pair_ref,
    mask_ref,
    gain_ref,
    shift_ref,
    bwt_ref,
    wqg_ref,
    wkv_ref,
    gb_ref,
    ow_ref,
    ob_ref,
    out_ref,
    own_ref,
    pay_ref,
    rows_buf,
    pieces,
    bias_buf,
    norm_send,
    norm_recv,
    local_sem,
    bias_send,
    bias_recv,
    fwd_sem,
):
    col_count = lax.axis_size("cols")
    row_count = lax.axis_size("rows")
    group = row_count // col_count
    me_r = lax.axis_index("rows")
    me_c = lax.axis_index("cols")
    own_rows, width, channels = pair_ref.shape
    depth = own_rows
    chunk = own_rows // CHUNKS
    mesh_id = pl.DeviceIdType.MESH
    target_c = me_r // group
    is_home = target_c == me_c
    parity = lax.rem(me_r, 2)
    half = row_count // 2
    sibling = me_r + 1 - 2 * parity
    barrier = pltpu.get_barrier_semaphore()
    for p in range(1, col_count):
        pl.semaphore_signal(
            barrier, 1, device_id=(me_r, lax.rem(me_c + p, col_count)), device_id_type=mesh_id
        )
    pl.semaphore_signal(barrier, 1, device_id=(sibling, me_c), device_id_type=mesh_id)
    for t in range(half):
        r = 2 * t + parity

        @pl.when(jnp.logical_not(jnp.logical_and(is_home, me_r == r)))
        def _():
            pl.semaphore_signal(barrier, 1, device_id=(r, target_c), device_id_type=mesh_id)

    for u in range(group // 2):
        for c in range(col_count):
            source = group * me_c + 2 * u + parity

            @pl.when(jnp.logical_not(jnp.logical_and(source == me_r, me_c == c)))
            def _():
                pl.semaphore_signal(barrier, 1, device_id=(source, c), device_id_type=mesh_id)

    as_float = pair_ref[...].astype(jnp.float32)
    center = jnp.mean(as_float, axis=-1, keepdims=True)
    spread = jnp.mean(jnp.square(as_float - center), axis=-1, keepdims=True)
    normed = (
        (as_float - center) * lax.rsqrt(spread + 1e-05) * gain_ref[...] + shift_ref[...]
    ).astype(jnp.bfloat16)
    own_ref[...] = normed
    flat = normed.reshape(own_rows * width, channels)
    bias_t = lax.dot_general(
        bwt_ref[...], flat, (((1,), (1,)), ((), ())), preferred_element_type=jnp.float32
    ).astype(jnp.bfloat16)
    mask_row = mask_ref[...].astype(jnp.float32).astype(jnp.bfloat16)
    for h in range(head_count):
        for j in range(own_rows):
            pay_ref[j : j + 1, h * width : (h + 1) * width] = bias_t[
                h : h + 1, j * width : (j + 1) * width
            ]
        pay_ref[own_rows : own_rows + 1, h * width : (h + 1) * width] = mask_row

    pl.semaphore_wait(barrier, col_count + 2 * (half - is_home.astype(jnp.int32)))

    block = lax.rem(me_r, group)
    slot = lax.rem(block, 2) * half + (block // 2) * col_count + me_c
    local_bias = pltpu.make_async_copy(pay_ref, pieces.at[slot], bias_recv)
    bias_copies = []
    for t in range(half):
        r = 2 * t + parity
        is_self = jnp.logical_and(is_home, me_r == r)
        copy = pltpu.make_async_remote_copy(
            src_ref=pay_ref,
            dst_ref=pieces.at[slot],
            send_sem=bias_send.at[t],
            recv_sem=bias_recv,
            device_id=(r, target_c),
            device_id_type=mesh_id,
        )

        @pl.when(jnp.logical_not(is_self))
        def _():
            copy.start()

        @pl.when(is_self)
        def _():
            local_bias.start()

        bias_copies.append((is_self, copy))

    home = pl.ds(pl.multiple_of(me_c * width, width), width)
    norm_copies = []
    locals_ = []
    for q in range(CHUNKS):
        part = pl.ds(q * chunk, chunk)
        local = pltpu.make_async_copy(own_ref.at[part], rows_buf.at[part, home, :], local_sem.at[q])
        local.start()
        locals_.append(local)
        for p in range(1, col_count):
            copy = pltpu.make_async_remote_copy(
                src_ref=own_ref.at[part],
                dst_ref=rows_buf.at[part, home, :],
                send_sem=norm_send.at[q, p],
                recv_sem=norm_recv.at[q],
                device_id=(me_r, lax.rem(me_c + p, col_count)),
                device_id_type=mesh_id,
            )
            copy.start()
            norm_copies.append(copy)

    direct = pieces.at[pl.ds(pl.multiple_of(parity * half, half), half)]
    pltpu.make_async_copy(direct, direct, bias_recv).wait()
    forward = pltpu.make_async_remote_copy(
        src_ref=direct,
        dst_ref=direct,
        send_sem=fwd_sem.at[0],
        recv_sem=fwd_sem.at[1],
        device_id=(sibling, me_c),
        device_id_type=mesh_id,
    )
    forward.start()
    forward.wait()
    for c in range(col_count):
        for m in range(group):
            piece = pieces[(m % 2) * half + (m // 2) * col_count + c].astype(jnp.float32)
            for h in range(head_count):
                bias_buf[h, m * depth : (m + 1) * depth, c * width : (c + 1) * width] = piece[
                    :depth, h * width : (h + 1) * width
                ]
            if m == 0:
                bias_buf[head_count, 0:1, c * width : (c + 1) * width] = piece[
                    depth : depth + 1, 0:width
                ]
    masking = 1000000000.0 * (bias_buf[head_count, 0:1, :] - 1.0)
    inner = ow_ref.shape[0]
    head_size = inner // head_count

    for q in range(CHUNKS):
        locals_[q].wait()
        arrived = pl.ds(0, (col_count - 1) * width)
        pltpu.make_async_copy(
            rows_buf.at[pl.ds(q * chunk, chunk), arrived, :],
            rows_buf.at[pl.ds(q * chunk, chunk), arrived, :],
            norm_recv.at[q],
        ).wait()

        def body(i, carry):
            updated = row_update(
                own_ref[i],
                rows_buf[i],
                bias_buf,
                masking,
                wqg_ref[...],
                wkv_ref[...],
                gb_ref[...],
                ow_ref[...],
                ob_ref[...],
                head_count,
                head_size,
            )
            out_ref[i] = updated.astype(out_ref.dtype)
            return carry

        lax.fori_loop(q * chunk, (q + 1) * chunk, body, 0)

    for copy in norm_copies:
        copy.wait_send()
    for is_self, copy in bias_copies:

        @pl.when(jnp.logical_not(is_self))
        def _():
            copy.wait_send()


def fused(pair, token_mask, norm_gain, norm_shift, bias_weight, wqg, wkv, gate_bias, out_weight, out_bias):
    own_rows, width, channels = pair.shape
    cols = lax.axis_size("cols")
    rows = lax.axis_size("rows")
    head_count = bias_weight.shape[1]
    slots = head_count + 1
    depth = own_rows
    group = rows // cols
    inner = out_weight.shape[0]
    vmem = pl.BlockSpec(memory_space=pltpu.VMEM)
    payload_shape = (own_rows + 1, head_count * width)
    return pl.pallas_call(
        functools.partial(fused_kernel, head_count),
        out_shape=jax.ShapeDtypeStruct(pair.shape, jnp.bfloat16),
        in_specs=[vmem] * 10,
        out_specs=vmem,
        scratch_shapes=[
            pltpu.VMEM(pair.shape, jnp.bfloat16),
            pltpu.VMEM(payload_shape, jnp.bfloat16),
            pltpu.VMEM((own_rows, cols * width, channels), jnp.bfloat16),
            pltpu.VMEM((rows,) + payload_shape, jnp.bfloat16),
            pltpu.VMEM((slots, group * depth, cols * width), jnp.float32),
            pltpu.SemaphoreType.DMA((CHUNKS, cols)),
            pltpu.SemaphoreType.DMA((CHUNKS,)),
            pltpu.SemaphoreType.DMA((CHUNKS,)),
            pltpu.SemaphoreType.DMA((rows // 2,)),
            pltpu.SemaphoreType.DMA(()),
            pltpu.SemaphoreType.DMA((2,)),
        ],
        compiler_params=pltpu.CompilerParams(
            has_side_effects=True, collective_id=0, vmem_limit_bytes=48 * 1024 * 1024
        ),
    )(
        pair,
        token_mask.reshape(1, width),
        norm_gain.reshape(1, channels),
        norm_shift.reshape(1, channels),
        bias_weight.T,
        wqg,
        wkv,
        gate_bias.reshape(1, inner),
        out_weight,
        out_bias.reshape(1, channels),
    )


def shards(
    pair, token_mask, norm_gain, norm_shift, in_weight, gate_bias, bias_weight, out_weight, out_bias
):
    inner = out_weight.shape[0]
    wqg = jnp.concatenate((in_weight[:, :inner], in_weight[:, 3 * inner :]), axis=1)
    wkv = in_weight[:, inner : 3 * inner]
    return fused(
        pair, token_mask, norm_gain, norm_shift, bias_weight, wqg, wkv, gate_bias, out_weight, out_bias
    )


def solution(mesh):
    placed = (P("rows", "cols", None), P("cols"), P(), P(), P(), P(), P(), P(), P())
    return jax.shard_map(
        shards, mesh=mesh, in_specs=placed, out_specs=P("rows", "cols", None), check_vma=False
    )
```

```python
import functools

import jax
import jax.numpy as jnp
from jax import lax
from jax.experimental import pallas as pl
from jax.experimental.pallas import tpu as pltpu
from jax.sharding import PartitionSpec as P


CHUNKS = 12


def row_update(own, row, bias_ref, masking, wqg, wkv, gb, ow, ob, head_count, head_size):
    inner = head_count * head_size
    qg = jnp.dot(own, wqg, preferred_element_type=jnp.float32)
    queries = (qg[:, :inner] * head_size ** (-0.5)).astype(jnp.bfloat16)
    gates = jax.nn.sigmoid(qg[:, inner:] + gb)
    keys_t = lax.dot_general(
        wkv[:, :inner], row, (((0,), (1,)), ((), ())), preferred_element_type=jnp.float32
    ).astype(jnp.bfloat16)
    values = jnp.dot(row, wkv[:, inner:], preferred_element_type=jnp.float32).astype(jnp.bfloat16)
    lane_head = lax.broadcasted_iota(jnp.int32, (1, inner), 1) // head_size
    queries_rows = own.shape[0]
    stacked = jnp.concatenate(
        [jnp.where(lane_head == h, queries, jnp.zeros_like(queries)) for h in range(head_count)],
        axis=0,
    )
    scores = jnp.dot(stacked, keys_t, preferred_element_type=jnp.float32)
    scores = scores + bias_ref[0:head_count].reshape(head_count * queries_rows, -1)
    scores = scores + masking
    top = jnp.max(scores, axis=-1, keepdims=True)
    expo = jnp.exp(scores - top)
    totals = jnp.sum(expo, axis=-1, keepdims=True)
    mixed = jnp.dot(expo.astype(jnp.bfloat16), values, preferred_element_type=jnp.float32)
    attended = jnp.zeros((queries_rows, inner), jnp.float32)
    for h in range(head_count):
        rows_h = slice(h * queries_rows, (h + 1) * queries_rows)
        attended = jnp.where(lane_head == h, mixed[rows_h] / totals[rows_h], attended)
    gated = (gates * attended).astype(jnp.bfloat16)
    return jnp.dot(gated, ow, preferred_element_type=jnp.float32) + ob


def fused_kernel(
    head_count,
    pair_ref,
    mask_ref,
    gain_ref,
    shift_ref,
    bwt_ref,
    wqg_ref,
    wkv_ref,
    gb_ref,
    ow_ref,
    ob_ref,
    out_ref,
    pair_buf,
    own_ref,
    pay_ref,
    rows_buf,
    pieces,
    bias_buf,
    norm_send,
    norm_recv,
    local_sem,
    bias_send,
    bias_recv,
    fwd_sem,
    pair_sem,
):
    col_count = lax.axis_size("cols")
    row_count = lax.axis_size("rows")
    group = row_count // col_count
    me_r = lax.axis_index("rows")
    me_c = lax.axis_index("cols")
    own_rows, width, channels = pair_ref.shape
    depth = own_rows
    chunk = own_rows // CHUNKS
    mesh_id = pl.DeviceIdType.MESH
    target_c = me_r // group
    is_home = target_c == me_c
    parity = lax.rem(me_r, 2)
    half = row_count // 2
    sibling = me_r + 1 - 2 * parity
    pair_in = pltpu.make_async_copy(pair_ref, pair_buf, pair_sem.at[0])
    pair_in.start()
    barrier = pltpu.get_barrier_semaphore()
    for p in range(1, col_count):
        pl.semaphore_signal(
            barrier, 1, device_id=(me_r, lax.rem(me_c + p, col_count)), device_id_type=mesh_id
        )
    pl.semaphore_signal(barrier, 1, device_id=(sibling, me_c), device_id_type=mesh_id)
    for t in range(half):
        r = 2 * t + parity

        @pl.when(jnp.logical_not(jnp.logical_and(is_home, me_r == r)))
        def _():
            pl.semaphore_signal(barrier, 1, device_id=(r, target_c), device_id_type=mesh_id)

    for u in range(group // 2):
        for c in range(col_count):
            source = group * me_c + 2 * u + parity

            @pl.when(jnp.logical_not(jnp.logical_and(source == me_r, me_c == c)))
            def _():
                pl.semaphore_signal(barrier, 1, device_id=(source, c), device_id_type=mesh_id)

    pair_in.wait()
    as_float = pair_buf[...].astype(jnp.float32)
    center = jnp.mean(as_float, axis=-1, keepdims=True)
    spread = jnp.mean(jnp.square(as_float - center), axis=-1, keepdims=True)
    normed = (
        (as_float - center) * lax.rsqrt(spread + 1e-05) * gain_ref[...] + shift_ref[...]
    ).astype(jnp.bfloat16)
    own_ref[...] = normed
    flat = normed.reshape(own_rows * width, channels)
    bias_t = lax.dot_general(
        bwt_ref[...], flat, (((1,), (1,)), ((), ())), preferred_element_type=jnp.float32
    ).astype(jnp.bfloat16)
    mask_row = mask_ref[...].astype(jnp.float32).astype(jnp.bfloat16)
    for h in range(head_count):
        for j in range(own_rows):
            pay_ref[j : j + 1, h * width : (h + 1) * width] = bias_t[
                h : h + 1, j * width : (j + 1) * width
            ]
        pay_ref[own_rows : own_rows + 1, h * width : (h + 1) * width] = mask_row

    pl.semaphore_wait(barrier, col_count + 2 * (half - is_home.astype(jnp.int32)))

    block = lax.rem(me_r, group)
    slot = lax.rem(block, 2) * half + (block // 2) * col_count + me_c
    local_bias = pltpu.make_async_copy(pay_ref, pieces.at[slot], bias_recv)
    bias_copies = []
    for t in range(half):
        r = 2 * t + parity
        is_self = jnp.logical_and(is_home, me_r == r)
        copy = pltpu.make_async_remote_copy(
            src_ref=pay_ref,
            dst_ref=pieces.at[slot],
            send_sem=bias_send.at[t],
            recv_sem=bias_recv,
            device_id=(r, target_c),
            device_id_type=mesh_id,
        )

        @pl.when(jnp.logical_not(is_self))
        def _():
            copy.start()

        @pl.when(is_self)
        def _():
            local_bias.start()

        bias_copies.append((is_self, copy))

    home = pl.ds(pl.multiple_of(me_c * width, width), width)
    norm_copies = []
    locals_ = []
    for q in range(CHUNKS):
        part = pl.ds(q * chunk, chunk)
        local = pltpu.make_async_copy(own_ref.at[part], rows_buf.at[part, home, :], local_sem.at[q])
        local.start()
        locals_.append(local)
        for p in range(1, col_count):
            copy = pltpu.make_async_remote_copy(
                src_ref=own_ref.at[part],
                dst_ref=rows_buf.at[part, home, :],
                send_sem=norm_send.at[q, p],
                recv_sem=norm_recv.at[q],
                device_id=(me_r, lax.rem(me_c + p, col_count)),
                device_id_type=mesh_id,
            )
            copy.start()
            norm_copies.append(copy)

    direct = pieces.at[pl.ds(pl.multiple_of(parity * half, half), half)]
    pltpu.make_async_copy(direct, direct, bias_recv).wait()
    forward = pltpu.make_async_remote_copy(
        src_ref=direct,
        dst_ref=direct,
        send_sem=fwd_sem.at[0],
        recv_sem=fwd_sem.at[1],
        device_id=(sibling, me_c),
        device_id_type=mesh_id,
    )
    forward.start()
    forward.wait()
    for c in range(col_count):
        for m in range(group):
            piece = pieces[(m % 2) * half + (m // 2) * col_count + c].astype(jnp.float32)
            for h in range(head_count):
                bias_buf[h, m * depth : (m + 1) * depth, c * width : (c + 1) * width] = piece[
                    :depth, h * width : (h + 1) * width
                ]
            if m == 0:
                bias_buf[head_count, 0:1, c * width : (c + 1) * width] = piece[
                    depth : depth + 1, 0:width
                ]
    masking = 1000000000.0 * (bias_buf[head_count, 0:1, :] - 1.0)
    inner = ow_ref.shape[0]
    head_size = inner // head_count

    for q in range(CHUNKS):
        locals_[q].wait()
        arrived = pl.ds(0, (col_count - 1) * width)
        pltpu.make_async_copy(
            rows_buf.at[pl.ds(q * chunk, chunk), arrived, :],
            rows_buf.at[pl.ds(q * chunk, chunk), arrived, :],
            norm_recv.at[q],
        ).wait()

        def body(i, carry):
            updated = row_update(
                own_ref[i],
                rows_buf[i],
                bias_buf,
                masking,
                wqg_ref[...],
                wkv_ref[...],
                gb_ref[...],
                ow_ref[...],
                ob_ref[...],
                head_count,
                head_size,
            )
            out_ref[i] = updated.astype(out_ref.dtype)
            return carry

        lax.fori_loop(q * chunk, (q + 1) * chunk, body, 0)

    for copy in norm_copies:
        copy.wait_send()
    for is_self, copy in bias_copies:

        @pl.when(jnp.logical_not(is_self))
        def _():
            copy.wait_send()


def fused(pair, token_mask, norm_gain, norm_shift, bias_weight, wqg, wkv, gate_bias, out_weight, out_bias):
    own_rows, width, channels = pair.shape
    cols = lax.axis_size("cols")
    rows = lax.axis_size("rows")
    head_count = bias_weight.shape[1]
    slots = head_count + 1
    depth = own_rows
    group = rows // cols
    inner = out_weight.shape[0]
    vmem = pl.BlockSpec(memory_space=pltpu.VMEM)
    payload_shape = (own_rows + 1, head_count * width)
    return pl.pallas_call(
        functools.partial(fused_kernel, head_count),
        out_shape=jax.ShapeDtypeStruct(pair.shape, jnp.bfloat16),
        in_specs=[pl.BlockSpec(memory_space=pl.ANY)] + [vmem] * 9,
        out_specs=vmem,
        scratch_shapes=[
            pltpu.VMEM(pair.shape, pair.dtype),
            pltpu.VMEM(pair.shape, jnp.bfloat16),
            pltpu.VMEM(payload_shape, jnp.bfloat16),
            pltpu.VMEM((own_rows, cols * width, channels), jnp.bfloat16),
            pltpu.VMEM((rows,) + payload_shape, jnp.bfloat16),
            pltpu.VMEM((slots, group * depth, cols * width), jnp.float32),
            pltpu.SemaphoreType.DMA((CHUNKS, cols)),
            pltpu.SemaphoreType.DMA((CHUNKS,)),
            pltpu.SemaphoreType.DMA((CHUNKS,)),
            pltpu.SemaphoreType.DMA((rows // 2,)),
            pltpu.SemaphoreType.DMA(()),
            pltpu.SemaphoreType.DMA((2,)),
            pltpu.SemaphoreType.DMA((1,)),
        ],
        compiler_params=pltpu.CompilerParams(
            has_side_effects=True, collective_id=0, vmem_limit_bytes=48 * 1024 * 1024
        ),
    )(
        pair,
        token_mask.reshape(1, width),
        norm_gain.reshape(1, channels),
        norm_shift.reshape(1, channels),
        bias_weight.T,
        wqg,
        wkv,
        gate_bias.reshape(1, inner),
        out_weight,
        out_bias.reshape(1, channels),
    )


def shards(
    pair, token_mask, norm_gain, norm_shift, in_weight, gate_bias, bias_weight, out_weight, out_bias
):
    inner = out_weight.shape[0]
    wqg = jnp.concatenate((in_weight[:, :inner], in_weight[:, 3 * inner :]), axis=1)
    wkv = in_weight[:, inner : 3 * inner]
    return fused(
        pair, token_mask, norm_gain, norm_shift, bias_weight, wqg, wkv, gate_bias, out_weight, out_bias
    )


def solution(mesh):
    placed = (P("rows", "cols", None), P("cols"), P(), P(), P(), P(), P(), P(), P())
    return jax.shard_map(
        shards, mesh=mesh, in_specs=placed, out_specs=P("rows", "cols", None), check_vma=False
    )
```

```python
import functools

import jax
import jax.numpy as jnp
from jax import lax
from jax.experimental import pallas as pl
from jax.experimental.pallas import tpu as pltpu
from jax.sharding import PartitionSpec as P


CHUNKS = 12


def row_update(own, row, bias_ref, masking, w_ref, gb, ow, ob, head_count, head_size):
    inner = head_count * head_size
    qp = jnp.dot(own, w_ref[:, :inner], preferred_element_type=jnp.float32)
    queries = (qp * head_size ** (-0.5)).astype(jnp.bfloat16)
    gp = jnp.dot(own, w_ref[:, 3 * inner :], preferred_element_type=jnp.float32)
    gates = jax.nn.sigmoid(gp + gb)
    keys_t = lax.dot_general(
        w_ref[:, inner : 2 * inner], row, (((0,), (1,)), ((), ())), preferred_element_type=jnp.float32
    ).astype(jnp.bfloat16)
    values = jnp.dot(
        row, w_ref[:, 2 * inner : 3 * inner], preferred_element_type=jnp.float32
    ).astype(jnp.bfloat16)
    lane_head = lax.broadcasted_iota(jnp.int32, (1, inner), 1) // head_size
    queries_rows = own.shape[0]
    stacked = jnp.concatenate(
        [jnp.where(lane_head == h, queries, jnp.zeros_like(queries)) for h in range(head_count)],
        axis=0,
    )
    scores = jnp.dot(stacked, keys_t, preferred_element_type=jnp.float32)
    scores = scores + bias_ref[0:head_count].reshape(head_count * queries_rows, -1)
    scores = scores + masking
    top = jnp.max(scores, axis=-1, keepdims=True)
    expo = jnp.exp(scores - top)
    totals = jnp.sum(expo, axis=-1, keepdims=True)
    mixed = jnp.dot(expo.astype(jnp.bfloat16), values, preferred_element_type=jnp.float32)
    attended = jnp.zeros((queries_rows, inner), jnp.float32)
    for h in range(head_count):
        rows_h = slice(h * queries_rows, (h + 1) * queries_rows)
        attended = jnp.where(lane_head == h, mixed[rows_h] / totals[rows_h], attended)
    gated = (gates * attended).astype(jnp.bfloat16)
    return jnp.dot(gated, ow, preferred_element_type=jnp.float32) + ob


def fused_kernel(
    head_count,
    pair_ref,
    mask_ref,
    gain_ref,
    shift_ref,
    bwt_ref,
    w_hbm,
    gb_ref,
    ow_hbm,
    ob_ref,
    out_ref,
    w_ref,
    ow_ref,
    pair_buf,
    own_ref,
    pay_ref,
    rows_buf,
    pieces,
    bias_buf,
    norm_send,
    norm_recv,
    local_sem,
    bias_send,
    bias_recv,
    fwd_sem,
    pair_sem,
):
    col_count = lax.axis_size("cols")
    row_count = lax.axis_size("rows")
    group = row_count // col_count
    me_r = lax.axis_index("rows")
    me_c = lax.axis_index("cols")
    own_rows, width, channels = pair_ref.shape
    depth = own_rows
    chunk = own_rows // CHUNKS
    mesh_id = pl.DeviceIdType.MESH
    target_c = me_r // group
    is_home = target_c == me_c
    parity = lax.rem(me_r, 2)
    half = row_count // 2
    sibling = me_r + 1 - 2 * parity
    pair_in = pltpu.make_async_copy(pair_ref, pair_buf, pair_sem.at[0])
    pair_in.start()
    w_in = pltpu.make_async_copy(w_hbm, w_ref, pair_sem.at[1])
    w_in.start()
    ow_in = pltpu.make_async_copy(ow_hbm, ow_ref, pair_sem.at[2])
    ow_in.start()
    barrier = pltpu.get_barrier_semaphore()
    for p in range(1, col_count):
        pl.semaphore_signal(
            barrier, 1, device_id=(me_r, lax.rem(me_c + p, col_count)), device_id_type=mesh_id
        )
    pl.semaphore_signal(barrier, 1, device_id=(sibling, me_c), device_id_type=mesh_id)
    for t in range(half):
        r = 2 * t + parity

        @pl.when(jnp.logical_not(jnp.logical_and(is_home, me_r == r)))
        def _():
            pl.semaphore_signal(barrier, 1, device_id=(r, target_c), device_id_type=mesh_id)

    for u in range(group // 2):
        for c in range(col_count):
            source = group * me_c + 2 * u + parity

            @pl.when(jnp.logical_not(jnp.logical_and(source == me_r, me_c == c)))
            def _():
                pl.semaphore_signal(barrier, 1, device_id=(source, c), device_id_type=mesh_id)

    pair_in.wait()
    as_float = pair_buf[...].astype(jnp.float32)
    center = jnp.mean(as_float, axis=-1, keepdims=True)
    spread = jnp.mean(jnp.square(as_float - center), axis=-1, keepdims=True)
    normed = (
        (as_float - center) * lax.rsqrt(spread + 1e-05) * gain_ref[...] + shift_ref[...]
    ).astype(jnp.bfloat16)
    own_ref[...] = normed
    flat = normed.reshape(own_rows * width, channels)
    bias_t = lax.dot_general(
        bwt_ref[...], flat, (((1,), (1,)), ((), ())), preferred_element_type=jnp.float32
    ).astype(jnp.bfloat16)
    mask_row = mask_ref[...].astype(jnp.float32).astype(jnp.bfloat16)
    for h in range(head_count):
        for j in range(own_rows):
            pay_ref[j : j + 1, h * width : (h + 1) * width] = bias_t[
                h : h + 1, j * width : (j + 1) * width
            ]
        pay_ref[own_rows : own_rows + 1, h * width : (h + 1) * width] = mask_row

    pl.semaphore_wait(barrier, col_count + 2 * (half - is_home.astype(jnp.int32)))

    block = lax.rem(me_r, group)
    slot = lax.rem(block, 2) * half + (block // 2) * col_count + me_c
    local_bias = pltpu.make_async_copy(pay_ref, pieces.at[slot], bias_recv)
    bias_copies = []
    for t in range(half):
        r = 2 * t + parity
        is_self = jnp.logical_and(is_home, me_r == r)
        copy = pltpu.make_async_remote_copy(
            src_ref=pay_ref,
            dst_ref=pieces.at[slot],
            send_sem=bias_send.at[t],
            recv_sem=bias_recv,
            device_id=(r, target_c),
            device_id_type=mesh_id,
        )

        @pl.when(jnp.logical_not(is_self))
        def _():
            copy.start()

        @pl.when(is_self)
        def _():
            local_bias.start()

        bias_copies.append((is_self, copy))

    home = pl.ds(pl.multiple_of(me_c * width, width), width)
    norm_copies = []
    locals_ = []
    for q in range(CHUNKS):
        part = pl.ds(q * chunk, chunk)
        local = pltpu.make_async_copy(own_ref.at[part], rows_buf.at[part, home, :], local_sem.at[q])
        local.start()
        locals_.append(local)
        for p in range(1, col_count):
            copy = pltpu.make_async_remote_copy(
                src_ref=own_ref.at[part],
                dst_ref=rows_buf.at[part, home, :],
                send_sem=norm_send.at[q, p],
                recv_sem=norm_recv.at[q],
                device_id=(me_r, lax.rem(me_c + p, col_count)),
                device_id_type=mesh_id,
            )
            copy.start()
            norm_copies.append(copy)

    direct = pieces.at[pl.ds(pl.multiple_of(parity * half, half), half)]
    pltpu.make_async_copy(direct, direct, bias_recv).wait()
    forward = pltpu.make_async_remote_copy(
        src_ref=direct,
        dst_ref=direct,
        send_sem=fwd_sem.at[0],
        recv_sem=fwd_sem.at[1],
        device_id=(sibling, me_c),
        device_id_type=mesh_id,
    )
    forward.start()
    forward.wait()
    for c in range(col_count):
        for m in range(group):
            piece = pieces[(m % 2) * half + (m // 2) * col_count + c].astype(jnp.float32)
            for h in range(head_count):
                bias_buf[h, m * depth : (m + 1) * depth, c * width : (c + 1) * width] = piece[
                    :depth, h * width : (h + 1) * width
                ]
            if m == 0:
                bias_buf[head_count, 0:1, c * width : (c + 1) * width] = piece[
                    depth : depth + 1, 0:width
                ]
    masking = 1000000000.0 * (bias_buf[head_count, 0:1, :] - 1.0)
    w_in.wait()
    ow_in.wait()
    inner = ow_ref.shape[0]
    head_size = inner // head_count

    for q in range(CHUNKS):
        locals_[q].wait()
        arrived = pl.ds(0, (col_count - 1) * width)
        pltpu.make_async_copy(
            rows_buf.at[pl.ds(q * chunk, chunk), arrived, :],
            rows_buf.at[pl.ds(q * chunk, chunk), arrived, :],
            norm_recv.at[q],
        ).wait()

        def body(i, carry):
            updated = row_update(
                own_ref[i],
                rows_buf[i],
                bias_buf,
                masking,
                w_ref,
                gb_ref[...],
                ow_ref[...],
                ob_ref[...],
                head_count,
                head_size,
            )
            out_ref[i] = updated.astype(out_ref.dtype)
            return carry

        lax.fori_loop(q * chunk, (q + 1) * chunk, body, 0)

    for copy in norm_copies:
        copy.wait_send()
    for is_self, copy in bias_copies:

        @pl.when(jnp.logical_not(is_self))
        def _():
            copy.wait_send()


def fused(pair, token_mask, norm_gain, norm_shift, bias_weight, in_weight, gate_bias, out_weight, out_bias):
    own_rows, width, channels = pair.shape
    cols = lax.axis_size("cols")
    rows = lax.axis_size("rows")
    head_count = bias_weight.shape[1]
    slots = head_count + 1
    depth = own_rows
    group = rows // cols
    inner = out_weight.shape[0]
    vmem = pl.BlockSpec(memory_space=pltpu.VMEM)
    any_spec = pl.BlockSpec(memory_space=pl.ANY)
    payload_shape = (own_rows + 1, head_count * width)
    return pl.pallas_call(
        functools.partial(fused_kernel, head_count),
        out_shape=jax.ShapeDtypeStruct(pair.shape, jnp.bfloat16),
        in_specs=[any_spec] + [vmem] * 4 + [any_spec, vmem, any_spec, vmem],
        out_specs=vmem,
        scratch_shapes=[
            pltpu.VMEM(in_weight.shape, in_weight.dtype),
            pltpu.VMEM(out_weight.shape, out_weight.dtype),
            pltpu.VMEM(pair.shape, pair.dtype),
            pltpu.VMEM(pair.shape, jnp.bfloat16),
            pltpu.VMEM(payload_shape, jnp.bfloat16),
            pltpu.VMEM((own_rows, cols * width, channels), jnp.bfloat16),
            pltpu.VMEM((rows,) + payload_shape, jnp.bfloat16),
            pltpu.VMEM((slots, group * depth, cols * width), jnp.float32),
            pltpu.SemaphoreType.DMA((CHUNKS, cols)),
            pltpu.SemaphoreType.DMA((CHUNKS,)),
            pltpu.SemaphoreType.DMA((CHUNKS,)),
            pltpu.SemaphoreType.DMA((rows // 2,)),
            pltpu.SemaphoreType.DMA(()),
            pltpu.SemaphoreType.DMA((2,)),
            pltpu.SemaphoreType.DMA((3,)),
        ],
        compiler_params=pltpu.CompilerParams(
            has_side_effects=True, collective_id=0, vmem_limit_bytes=48 * 1024 * 1024
        ),
    )(
        pair,
        token_mask.reshape(1, width),
        norm_gain.reshape(1, channels),
        norm_shift.reshape(1, channels),
        bias_weight.T,
        in_weight,
        gate_bias.reshape(1, inner),
        out_weight,
        out_bias.reshape(1, channels),
    )


def shards(
    pair, token_mask, norm_gain, norm_shift, in_weight, gate_bias, bias_weight, out_weight, out_bias
):
    return fused(
        pair, token_mask, norm_gain, norm_shift, bias_weight, in_weight, gate_bias, out_weight, out_bias
    )


def solution(mesh):
    placed = (P("rows", "cols", None), P("cols"), P(), P(), P(), P(), P(), P(), P())
    return jax.shard_map(
        shards, mesh=mesh, in_specs=placed, out_specs=P("rows", "cols", None), check_vma=False
    )
```

```python
import functools

import jax
import jax.numpy as jnp
from jax import lax
from jax.experimental import pallas as pl
from jax.experimental.pallas import tpu as pltpu
from jax.sharding import PartitionSpec as P


CHUNKS = 12


def row_update(own, row, bias_ref, masking, w_ref, gb, ow, ob, head_count, head_size):
    inner = head_count * head_size
    qp = jnp.dot(own, w_ref[:, :inner], preferred_element_type=jnp.float32)
    queries = (qp * head_size ** (-0.5)).astype(jnp.bfloat16)
    gp = jnp.dot(own, w_ref[:, 3 * inner :], preferred_element_type=jnp.float32)
    gates = jax.nn.sigmoid(gp + gb)
    keys_t = lax.dot_general(
        w_ref[:, inner : 2 * inner], row, (((0,), (1,)), ((), ())), preferred_element_type=jnp.float32
    ).astype(jnp.bfloat16)
    values = jnp.dot(
        row, w_ref[:, 2 * inner : 3 * inner], preferred_element_type=jnp.float32
    ).astype(jnp.bfloat16)
    lane_head = lax.broadcasted_iota(jnp.int32, (1, inner), 1) // head_size
    queries_rows = own.shape[0]
    stacked = jnp.concatenate(
        [jnp.where(lane_head == h, queries, jnp.zeros_like(queries)) for h in range(head_count)],
        axis=0,
    )
    scores = jnp.dot(stacked, keys_t, preferred_element_type=jnp.float32)
    scores = scores + bias_ref[0:head_count].reshape(head_count * queries_rows, -1)
    scores = scores + masking
    top = jnp.max(scores, axis=-1, keepdims=True)
    expo = jnp.exp(scores - top)
    totals = jnp.sum(expo, axis=-1, keepdims=True)
    mixed = jnp.dot(expo.astype(jnp.bfloat16), values, preferred_element_type=jnp.float32)
    attended = jnp.zeros((queries_rows, inner), jnp.float32)
    for h in range(head_count):
        rows_h = slice(h * queries_rows, (h + 1) * queries_rows)
        attended = jnp.where(lane_head == h, mixed[rows_h] / totals[rows_h], attended)
    gated = (gates * attended).astype(jnp.bfloat16)
    return jnp.dot(gated, ow, preferred_element_type=jnp.float32) + ob


def fused_kernel(
    head_count,
    pair_ref,
    mask_hbm,
    gain_hbm,
    shift_hbm,
    bwt_hbm,
    w_hbm,
    gb_hbm,
    ow_hbm,
    ob_hbm,
    out_ref,
    mask_ref,
    gain_ref,
    shift_ref,
    bwt_ref,
    gb_ref,
    ob_ref,
    small_sem,
    w_ref,
    ow_ref,
    pair_buf,
    own_ref,
    pay_ref,
    rows_buf,
    pieces,
    bias_buf,
    norm_send,
    norm_recv,
    local_sem,
    bias_send,
    bias_recv,
    fwd_sem,
    pair_sem,
):
    col_count = lax.axis_size("cols")
    row_count = lax.axis_size("rows")
    group = row_count // col_count
    me_r = lax.axis_index("rows")
    me_c = lax.axis_index("cols")
    own_rows, width, channels = pair_ref.shape
    depth = own_rows
    chunk = own_rows // CHUNKS
    mesh_id = pl.DeviceIdType.MESH
    target_c = me_r // group
    is_home = target_c == me_c
    parity = lax.rem(me_r, 2)
    half = row_count // 2
    sibling = me_r + 1 - 2 * parity
    pair_in = pltpu.make_async_copy(pair_ref, pair_buf, pair_sem.at[0])
    pair_in.start()
    w_in = pltpu.make_async_copy(w_hbm, w_ref, pair_sem.at[1])
    w_in.start()
    ow_in = pltpu.make_async_copy(ow_hbm, ow_ref, pair_sem.at[2])
    ow_in.start()
    small_in = []
    for n, (src, dst) in enumerate(
        (
            (mask_hbm, mask_ref),
            (gain_hbm, gain_ref),
            (shift_hbm, shift_ref),
            (bwt_hbm, bwt_ref),
            (gb_hbm, gb_ref),
            (ob_hbm, ob_ref),
        )
    ):
        small = pltpu.make_async_copy(src, dst, small_sem.at[n])
        small.start()
        small_in.append(small)
    barrier = pltpu.get_barrier_semaphore()
    for p in range(1, col_count):
        pl.semaphore_signal(
            barrier, 1, device_id=(me_r, lax.rem(me_c + p, col_count)), device_id_type=mesh_id
        )
    pl.semaphore_signal(barrier, 1, device_id=(sibling, me_c), device_id_type=mesh_id)
    for t in range(half):
        r = 2 * t + parity

        @pl.when(jnp.logical_not(jnp.logical_and(is_home, me_r == r)))
        def _():
            pl.semaphore_signal(barrier, 1, device_id=(r, target_c), device_id_type=mesh_id)

    for u in range(group // 2):
        for c in range(col_count):
            source = group * me_c + 2 * u + parity

            @pl.when(jnp.logical_not(jnp.logical_and(source == me_r, me_c == c)))
            def _():
                pl.semaphore_signal(barrier, 1, device_id=(source, c), device_id_type=mesh_id)

    pair_in.wait()
    for small in small_in:
        small.wait()
    as_float = pair_buf[...].astype(jnp.float32)
    center = jnp.mean(as_float, axis=-1, keepdims=True)
    spread = jnp.mean(jnp.square(as_float - center), axis=-1, keepdims=True)
    normed = (
        (as_float - center) * lax.rsqrt(spread + 1e-05) * gain_ref[...] + shift_ref[...]
    ).astype(jnp.bfloat16)
    own_ref[...] = normed
    flat = normed.reshape(own_rows * width, channels)
    bias_t = lax.dot_general(
        bwt_ref[...], flat, (((1,), (1,)), ((), ())), preferred_element_type=jnp.float32
    ).astype(jnp.bfloat16)
    mask_row = mask_ref[...].astype(jnp.float32).astype(jnp.bfloat16)
    for h in range(head_count):
        for j in range(own_rows):
            pay_ref[j : j + 1, h * width : (h + 1) * width] = bias_t[
                h : h + 1, j * width : (j + 1) * width
            ]
        pay_ref[own_rows : own_rows + 1, h * width : (h + 1) * width] = mask_row

    pl.semaphore_wait(barrier, col_count + 2 * (half - is_home.astype(jnp.int32)))

    block = lax.rem(me_r, group)
    slot = lax.rem(block, 2) * half + (block // 2) * col_count + me_c
    local_bias = pltpu.make_async_copy(pay_ref, pieces.at[slot], bias_recv)
    bias_copies = []
    for t in range(half):
        r = 2 * t + parity
        is_self = jnp.logical_and(is_home, me_r == r)
        copy = pltpu.make_async_remote_copy(
            src_ref=pay_ref,
            dst_ref=pieces.at[slot],
            send_sem=bias_send.at[t],
            recv_sem=bias_recv,
            device_id=(r, target_c),
            device_id_type=mesh_id,
        )

        @pl.when(jnp.logical_not(is_self))
        def _():
            copy.start()

        @pl.when(is_self)
        def _():
            local_bias.start()

        bias_copies.append((is_self, copy))

    home = pl.ds(pl.multiple_of(me_c * width, width), width)
    norm_copies = []
    locals_ = []
    for q in range(CHUNKS):
        part = pl.ds(q * chunk, chunk)
        local = pltpu.make_async_copy(own_ref.at[part], rows_buf.at[part, home, :], local_sem.at[q])
        local.start()
        locals_.append(local)
        for p in range(1, col_count):
            copy = pltpu.make_async_remote_copy(
                src_ref=own_ref.at[part],
                dst_ref=rows_buf.at[part, home, :],
                send_sem=norm_send.at[q, p],
                recv_sem=norm_recv.at[q],
                device_id=(me_r, lax.rem(me_c + p, col_count)),
                device_id_type=mesh_id,
            )
            copy.start()
            norm_copies.append(copy)

    direct = pieces.at[pl.ds(pl.multiple_of(parity * half, half), half)]
    pltpu.make_async_copy(direct, direct, bias_recv).wait()
    forward = pltpu.make_async_remote_copy(
        src_ref=direct,
        dst_ref=direct,
        send_sem=fwd_sem.at[0],
        recv_sem=fwd_sem.at[1],
        device_id=(sibling, me_c),
        device_id_type=mesh_id,
    )
    forward.start()
    forward.wait()
    for c in range(col_count):
        for m in range(group):
            piece = pieces[(m % 2) * half + (m // 2) * col_count + c].astype(jnp.float32)
            for h in range(head_count):
                bias_buf[h, m * depth : (m + 1) * depth, c * width : (c + 1) * width] = piece[
                    :depth, h * width : (h + 1) * width
                ]
            if m == 0:
                bias_buf[head_count, 0:1, c * width : (c + 1) * width] = piece[
                    depth : depth + 1, 0:width
                ]
    masking = 1000000000.0 * (bias_buf[head_count, 0:1, :] - 1.0)
    w_in.wait()
    ow_in.wait()
    inner = ow_ref.shape[0]
    head_size = inner // head_count

    for q in range(CHUNKS):
        locals_[q].wait()
        arrived = pl.ds(0, (col_count - 1) * width)
        pltpu.make_async_copy(
            rows_buf.at[pl.ds(q * chunk, chunk), arrived, :],
            rows_buf.at[pl.ds(q * chunk, chunk), arrived, :],
            norm_recv.at[q],
        ).wait()

        def body(i, carry):
            updated = row_update(
                own_ref[i],
                rows_buf[i],
                bias_buf,
                masking,
                w_ref,
                gb_ref[...],
                ow_ref[...],
                ob_ref[...],
                head_count,
                head_size,
            )
            out_ref[i] = updated.astype(out_ref.dtype)
            return carry

        lax.fori_loop(q * chunk, (q + 1) * chunk, body, 0)

    for copy in norm_copies:
        copy.wait_send()
    for is_self, copy in bias_copies:

        @pl.when(jnp.logical_not(is_self))
        def _():
            copy.wait_send()


def fused(pair, token_mask, norm_gain, norm_shift, bias_weight, in_weight, gate_bias, out_weight, out_bias):
    own_rows, width, channels = pair.shape
    cols = lax.axis_size("cols")
    rows = lax.axis_size("rows")
    head_count = bias_weight.shape[1]
    slots = head_count + 1
    depth = own_rows
    group = rows // cols
    inner = out_weight.shape[0]
    vmem = pl.BlockSpec(memory_space=pltpu.VMEM)
    any_spec = pl.BlockSpec(memory_space=pl.ANY)
    payload_shape = (own_rows + 1, head_count * width)
    return pl.pallas_call(
        functools.partial(fused_kernel, head_count),
        out_shape=jax.ShapeDtypeStruct(pair.shape, jnp.bfloat16),
        in_specs=[any_spec] * 9,
        out_specs=vmem,
        scratch_shapes=[
            pltpu.VMEM((1, width), token_mask.dtype),
            pltpu.VMEM((1, channels), norm_gain.dtype),
            pltpu.VMEM((1, channels), norm_shift.dtype),
            pltpu.VMEM((head_count, channels), bias_weight.dtype),
            pltpu.VMEM((1, inner), gate_bias.dtype),
            pltpu.VMEM((1, channels), out_bias.dtype),
            pltpu.SemaphoreType.DMA((6,)),
            pltpu.VMEM(in_weight.shape, in_weight.dtype),
            pltpu.VMEM(out_weight.shape, out_weight.dtype),
            pltpu.VMEM(pair.shape, pair.dtype),
            pltpu.VMEM(pair.shape, jnp.bfloat16),
            pltpu.VMEM(payload_shape, jnp.bfloat16),
            pltpu.VMEM((own_rows, cols * width, channels), jnp.bfloat16),
            pltpu.VMEM((rows,) + payload_shape, jnp.bfloat16),
            pltpu.VMEM((slots, group * depth, cols * width), jnp.float32),
            pltpu.SemaphoreType.DMA((CHUNKS, cols)),
            pltpu.SemaphoreType.DMA((CHUNKS,)),
            pltpu.SemaphoreType.DMA((CHUNKS,)),
            pltpu.SemaphoreType.DMA((rows // 2,)),
            pltpu.SemaphoreType.DMA(()),
            pltpu.SemaphoreType.DMA((2,)),
            pltpu.SemaphoreType.DMA((3,)),
        ],
        compiler_params=pltpu.CompilerParams(
            has_side_effects=True, collective_id=0, vmem_limit_bytes=48 * 1024 * 1024
        ),
    )(
        pair,
        token_mask.reshape(1, width),
        norm_gain.reshape(1, channels),
        norm_shift.reshape(1, channels),
        bias_weight.T,
        in_weight,
        gate_bias.reshape(1, inner),
        out_weight,
        out_bias.reshape(1, channels),
    )


def shards(
    pair, token_mask, norm_gain, norm_shift, in_weight, gate_bias, bias_weight, out_weight, out_bias
):
    return fused(
        pair, token_mask, norm_gain, norm_shift, bias_weight, in_weight, gate_bias, out_weight, out_bias
    )


def solution(mesh):
    placed = (P("rows", "cols", None), P("cols"), P(), P(), P(), P(), P(), P(), P())
    return jax.shard_map(
        shards, mesh=mesh, in_specs=placed, out_specs=P("rows", "cols", None), check_vma=False
    )
```

```python
import functools

import jax
import jax.numpy as jnp
from jax import lax
from jax.experimental import pallas as pl
from jax.experimental.pallas import tpu as pltpu
from jax.sharding import PartitionSpec as P


CHUNKS = 24


def row_update(own, row, bias_ref, masking, wqg, wkv, gb, ow, ob, head_count, head_size):
    inner = head_count * head_size
    qg = jnp.dot(own, wqg, preferred_element_type=jnp.float32)
    queries = (qg[:, :inner] * head_size ** (-0.5)).astype(jnp.bfloat16)
    gates = jax.nn.sigmoid(qg[:, inner:] + gb)
    keys_t = lax.dot_general(
        wkv[:, :inner], row, (((0,), (1,)), ((), ())), preferred_element_type=jnp.float32
    ).astype(jnp.bfloat16)
    values = jnp.dot(row, wkv[:, inner:], preferred_element_type=jnp.float32).astype(jnp.bfloat16)
    lane_head = lax.broadcasted_iota(jnp.int32, (1, inner), 1) // head_size
    queries_rows = own.shape[0]
    stacked = jnp.concatenate(
        [jnp.where(lane_head == h, queries, jnp.zeros_like(queries)) for h in range(head_count)],
        axis=0,
    )
    scores = jnp.dot(stacked, keys_t, preferred_element_type=jnp.float32)
    scores = scores + bias_ref[0:head_count].reshape(head_count * queries_rows, -1)
    scores = scores + masking
    top = jnp.max(scores, axis=-1, keepdims=True)
    expo = jnp.exp(scores - top)
    totals = jnp.sum(expo, axis=-1, keepdims=True)
    mixed = jnp.dot(expo.astype(jnp.bfloat16), values, preferred_element_type=jnp.float32)
    attended = jnp.zeros((queries_rows, inner), jnp.float32)
    for h in range(head_count):
        rows_h = slice(h * queries_rows, (h + 1) * queries_rows)
        attended = jnp.where(lane_head == h, mixed[rows_h] / totals[rows_h], attended)
    gated = (gates * attended).astype(jnp.bfloat16)
    return jnp.dot(gated, ow, preferred_element_type=jnp.float32) + ob


def fused_kernel(
    head_count,
    pair_ref,
    mask_ref,
    gain_ref,
    shift_ref,
    bwt_ref,
    wqg_ref,
    wkv_ref,
    gb_ref,
    ow_ref,
    ob_ref,
    out_ref,
    own_ref,
    pay_ref,
    rows_buf,
    pieces,
    bias_buf,
    norm_send,
    norm_recv,
    local_sem,
    bias_send,
    bias_recv,
    fwd_sem,
):
    col_count = lax.axis_size("cols")
    row_count = lax.axis_size("rows")
    group = row_count // col_count
    me_r = lax.axis_index("rows")
    me_c = lax.axis_index("cols")
    own_rows, width, channels = pair_ref.shape
    depth = own_rows
    chunk = own_rows // CHUNKS
    mesh_id = pl.DeviceIdType.MESH
    target_c = me_r // group
    is_home = target_c == me_c
    parity = lax.rem(me_r, 2)
    half = row_count // 2
    sibling = me_r + 1 - 2 * parity
    barrier = pltpu.get_barrier_semaphore()
    for p in range(1, col_count):
        pl.semaphore_signal(
            barrier, 1, device_id=(me_r, lax.rem(me_c + p, col_count)), device_id_type=mesh_id
        )
    pl.semaphore_signal(barrier, 1, device_id=(sibling, me_c), device_id_type=mesh_id)
    for t in range(half):
        r = 2 * t + parity

        @pl.when(jnp.logical_not(jnp.logical_and(is_home, me_r == r)))
        def _():
            pl.semaphore_signal(barrier, 1, device_id=(r, target_c), device_id_type=mesh_id)

    for u in range(group // 2):
        for c in range(col_count):
            source = group * me_c + 2 * u + parity

            @pl.when(jnp.logical_not(jnp.logical_and(source == me_r, me_c == c)))
            def _():
                pl.semaphore_signal(barrier, 1, device_id=(source, c), device_id_type=mesh_id)

    as_float = pair_ref[...].astype(jnp.float32)
    center = jnp.mean(as_float, axis=-1, keepdims=True)
    spread = jnp.mean(jnp.square(as_float - center), axis=-1, keepdims=True)
    normed = (
        (as_float - center) * lax.rsqrt(spread + 1e-05) * gain_ref[...] + shift_ref[...]
    ).astype(jnp.bfloat16)
    own_ref[...] = normed
    flat = normed.reshape(own_rows * width, channels)
    bias_t = lax.dot_general(
        bwt_ref[...], flat, (((1,), (1,)), ((), ())), preferred_element_type=jnp.float32
    ).astype(jnp.bfloat16)
    mask_row = mask_ref[...].astype(jnp.float32).astype(jnp.bfloat16)
    for h in range(head_count):
        for j in range(own_rows):
            pay_ref[j : j + 1, h * width : (h + 1) * width] = bias_t[
                h : h + 1, j * width : (j + 1) * width
            ]
        pay_ref[own_rows : own_rows + 1, h * width : (h + 1) * width] = mask_row

    pl.semaphore_wait(barrier, col_count + 2 * (half - is_home.astype(jnp.int32)))

    block = lax.rem(me_r, group)
    slot = lax.rem(block, 2) * half + (block // 2) * col_count + me_c
    local_bias = pltpu.make_async_copy(pay_ref, pieces.at[slot], bias_recv)
    bias_copies = []
    for t in range(half):
        r = 2 * t + parity
        is_self = jnp.logical_and(is_home, me_r == r)
        copy = pltpu.make_async_remote_copy(
            src_ref=pay_ref,
            dst_ref=pieces.at[slot],
            send_sem=bias_send.at[t],
            recv_sem=bias_recv,
            device_id=(r, target_c),
            device_id_type=mesh_id,
        )

        @pl.when(jnp.logical_not(is_self))
        def _():
            copy.start()

        @pl.when(is_self)
        def _():
            local_bias.start()

        bias_copies.append((is_self, copy))

    home = pl.ds(pl.multiple_of(me_c * width, width), width)
    norm_copies = []
    locals_ = []
    for q in range(CHUNKS):
        part = pl.ds(q * chunk, chunk)
        local = pltpu.make_async_copy(own_ref.at[part], rows_buf.at[part, home, :], local_sem.at[q])
        local.start()
        locals_.append(local)
        for p in range(1, col_count):
            copy = pltpu.make_async_remote_copy(
                src_ref=own_ref.at[part],
                dst_ref=rows_buf.at[part, home, :],
                send_sem=norm_send.at[q, p],
                recv_sem=norm_recv.at[q],
                device_id=(me_r, lax.rem(me_c + p, col_count)),
                device_id_type=mesh_id,
            )
            copy.start()
            norm_copies.append(copy)

    direct = pieces.at[pl.ds(pl.multiple_of(parity * half, half), half)]
    pltpu.make_async_copy(direct, direct, bias_recv).wait()
    forward = pltpu.make_async_remote_copy(
        src_ref=direct,
        dst_ref=direct,
        send_sem=fwd_sem.at[0],
        recv_sem=fwd_sem.at[1],
        device_id=(sibling, me_c),
        device_id_type=mesh_id,
    )
    forward.start()
    forward.wait()
    for c in range(col_count):
        for m in range(group):
            piece = pieces[(m % 2) * half + (m // 2) * col_count + c].astype(jnp.float32)
            for h in range(head_count):
                bias_buf[h, m * depth : (m + 1) * depth, c * width : (c + 1) * width] = piece[
                    :depth, h * width : (h + 1) * width
                ]
            if m == 0:
                bias_buf[head_count, 0:1, c * width : (c + 1) * width] = piece[
                    depth : depth + 1, 0:width
                ]
    masking = 1000000000.0 * (bias_buf[head_count, 0:1, :] - 1.0)
    inner = ow_ref.shape[0]
    head_size = inner // head_count

    for q in range(CHUNKS):
        locals_[q].wait()
        arrived = pl.ds(0, (col_count - 1) * width)
        pltpu.make_async_copy(
            rows_buf.at[pl.ds(q * chunk, chunk), arrived, :],
            rows_buf.at[pl.ds(q * chunk, chunk), arrived, :],
            norm_recv.at[q],
        ).wait()

        def body(i, carry):
            updated = row_update(
                own_ref[i],
                rows_buf[i],
                bias_buf,
                masking,
                wqg_ref[...],
                wkv_ref[...],
                gb_ref[...],
                ow_ref[...],
                ob_ref[...],
                head_count,
                head_size,
            )
            out_ref[i] = updated.astype(out_ref.dtype)
            return carry

        lax.fori_loop(q * chunk, (q + 1) * chunk, body, 0)

    for copy in norm_copies:
        copy.wait_send()
    for is_self, copy in bias_copies:

        @pl.when(jnp.logical_not(is_self))
        def _():
            copy.wait_send()


def fused(pair, token_mask, norm_gain, norm_shift, bias_weight, wqg, wkv, gate_bias, out_weight, out_bias):
    own_rows, width, channels = pair.shape
    cols = lax.axis_size("cols")
    rows = lax.axis_size("rows")
    head_count = bias_weight.shape[1]
    slots = head_count + 1
    depth = own_rows
    group = rows // cols
    inner = out_weight.shape[0]
    vmem = pl.BlockSpec(memory_space=pltpu.VMEM)
    payload_shape = (own_rows + 1, head_count * width)
    return pl.pallas_call(
        functools.partial(fused_kernel, head_count),
        out_shape=jax.ShapeDtypeStruct(pair.shape, jnp.bfloat16),
        in_specs=[vmem] * 10,
        out_specs=vmem,
        scratch_shapes=[
            pltpu.VMEM(pair.shape, jnp.bfloat16),
            pltpu.VMEM(payload_shape, jnp.bfloat16),
            pltpu.VMEM((own_rows, cols * width, channels), jnp.bfloat16),
            pltpu.VMEM((rows,) + payload_shape, jnp.bfloat16),
            pltpu.VMEM((slots, group * depth, cols * width), jnp.float32),
            pltpu.SemaphoreType.DMA((CHUNKS, cols)),
            pltpu.SemaphoreType.DMA((CHUNKS,)),
            pltpu.SemaphoreType.DMA((CHUNKS,)),
            pltpu.SemaphoreType.DMA((rows // 2,)),
            pltpu.SemaphoreType.DMA(()),
            pltpu.SemaphoreType.DMA((2,)),
        ],
        compiler_params=pltpu.CompilerParams(
            has_side_effects=True, collective_id=0, vmem_limit_bytes=48 * 1024 * 1024
        ),
    )(
        pair,
        token_mask.reshape(1, width),
        norm_gain.reshape(1, channels),
        norm_shift.reshape(1, channels),
        bias_weight.T,
        wqg,
        wkv,
        gate_bias.reshape(1, inner),
        out_weight,
        out_bias.reshape(1, channels),
    )


def shards(
    pair, token_mask, norm_gain, norm_shift, in_weight, gate_bias, bias_weight, out_weight, out_bias
):
    inner = out_weight.shape[0]
    wqg = jnp.concatenate((in_weight[:, :inner], in_weight[:, 3 * inner :]), axis=1)
    wkv = in_weight[:, inner : 3 * inner]
    return fused(
        pair, token_mask, norm_gain, norm_shift, bias_weight, wqg, wkv, gate_bias, out_weight, out_bias
    )


def solution(mesh):
    placed = (P("rows", "cols", None), P("cols"), P(), P(), P(), P(), P(), P(), P())
    return jax.shard_map(
        shards, mesh=mesh, in_specs=placed, out_specs=P("rows", "cols", None), check_vma=False
    )
```

```python
import functools

import jax
import jax.numpy as jnp
from jax import lax
from jax.experimental import pallas as pl
from jax.experimental.pallas import tpu as pltpu
from jax.sharding import PartitionSpec as P


CHUNKS = 12


def row_update(own, row, bias_ref, masking, wqg, wkv, gb, ow, ob, head_count, head_size):
    inner = head_count * head_size
    qg = jnp.dot(own, wqg, preferred_element_type=jnp.float32)
    queries = (qg[:, :inner] * head_size ** (-0.5)).astype(jnp.bfloat16)
    gates = jax.nn.sigmoid(qg[:, inner:] + gb)
    keys_t = lax.dot_general(
        wkv[:, :inner], row, (((0,), (1,)), ((), ())), preferred_element_type=jnp.float32
    ).astype(jnp.bfloat16)
    values = jnp.dot(row, wkv[:, inner:], preferred_element_type=jnp.float32).astype(jnp.bfloat16)
    lane_head = lax.broadcasted_iota(jnp.int32, (1, inner), 1) // head_size
    queries_rows = own.shape[0]
    stacked = jnp.concatenate(
        [jnp.where(lane_head == h, queries, jnp.zeros_like(queries)) for h in range(head_count)],
        axis=0,
    )
    scores = jnp.dot(stacked, keys_t, preferred_element_type=jnp.float32)
    scores = scores + bias_ref[0:head_count].reshape(head_count * queries_rows, -1)
    scores = scores + masking
    top = jnp.max(scores, axis=-1, keepdims=True)
    expo = jnp.exp(scores - top)
    totals = jnp.sum(expo, axis=-1, keepdims=True)
    mixed = jnp.dot(expo.astype(jnp.bfloat16), values, preferred_element_type=jnp.float32)
    attended = jnp.zeros((queries_rows, inner), jnp.float32)
    for h in range(head_count):
        rows_h = slice(h * queries_rows, (h + 1) * queries_rows)
        attended = jnp.where(lane_head == h, mixed[rows_h] / totals[rows_h], attended)
    gated = (gates * attended).astype(jnp.bfloat16)
    return jnp.dot(gated, ow, preferred_element_type=jnp.float32) + ob


def fused_kernel(
    head_count,
    pair_ref,
    mask_ref,
    gain_ref,
    shift_ref,
    bwt_ref,
    wqg_ref,
    wkv_ref,
    gb_ref,
    ow_ref,
    ob_ref,
    out_ref,
    own_ref,
    pay_ref,
    rows_buf,
    pieces,
    bias_buf,
    norm_send,
    norm_recv,
    local_sem,
    bias_send,
    bias_recv,
    fwd_sem,
):
    col_count = lax.axis_size("cols")
    row_count = lax.axis_size("rows")
    group = row_count // col_count
    me_r = lax.axis_index("rows")
    me_c = lax.axis_index("cols")
    own_rows, width, channels = pair_ref.shape
    depth = own_rows
    chunk = own_rows // CHUNKS
    mesh_id = pl.DeviceIdType.MESH
    target_c = me_r // group
    is_home = target_c == me_c
    parity = lax.rem(me_r, 2)
    half = row_count // 2
    sibling = me_r + 1 - 2 * parity
    barrier = pltpu.get_barrier_semaphore()
    for p in range(1, col_count):
        pl.semaphore_signal(
            barrier, 1, device_id=(me_r, lax.rem(me_c + p, col_count)), device_id_type=mesh_id
        )
    pl.semaphore_signal(barrier, 1, device_id=(sibling, me_c), device_id_type=mesh_id)
    for t in range(half):
        r = 2 * t + parity

        @pl.when(jnp.logical_not(jnp.logical_and(is_home, me_r == r)))
        def _():
            pl.semaphore_signal(barrier, 1, device_id=(r, target_c), device_id_type=mesh_id)

    for u in range(group // 2):
        for c in range(col_count):
            source = group * me_c + 2 * u + parity

            @pl.when(jnp.logical_not(jnp.logical_and(source == me_r, me_c == c)))
            def _():
                pl.semaphore_signal(barrier, 1, device_id=(source, c), device_id_type=mesh_id)

    as_float = pair_ref[...].astype(jnp.float32)
    center = jnp.mean(as_float, axis=-1, keepdims=True)
    spread = jnp.mean(jnp.square(as_float - center), axis=-1, keepdims=True)
    normed = (
        (as_float - center) * lax.rsqrt(spread + 1e-05) * gain_ref[...] + shift_ref[...]
    ).astype(jnp.bfloat16)
    own_ref[...] = normed
    flat = normed.reshape(own_rows * width, channels)
    bias_t = lax.dot_general(
        bwt_ref[...], flat, (((1,), (1,)), ((), ())), preferred_element_type=jnp.float32
    ).astype(jnp.bfloat16)
    mask_row = mask_ref[...].astype(jnp.float32).astype(jnp.bfloat16)
    for h in range(head_count):
        for j in range(own_rows):
            pay_ref[j : j + 1, h * width : (h + 1) * width] = bias_t[
                h : h + 1, j * width : (j + 1) * width
            ]
        pay_ref[own_rows : own_rows + 1, h * width : (h + 1) * width] = mask_row

    pl.semaphore_wait(barrier, col_count + 2 * (half - is_home.astype(jnp.int32)))

    block = lax.rem(me_r, group)
    slot = lax.rem(block, 2) * half + (block // 2) * col_count + me_c
    local_bias = pltpu.make_async_copy(pay_ref, pieces.at[slot], bias_recv)
    bias_copies = []
    for t in range(half):
        r = 2 * t + parity
        is_self = jnp.logical_and(is_home, me_r == r)
        copy = pltpu.make_async_remote_copy(
            src_ref=pay_ref,
            dst_ref=pieces.at[slot],
            send_sem=bias_send.at[t],
            recv_sem=bias_recv,
            device_id=(r, target_c),
            device_id_type=mesh_id,
        )

        @pl.when(jnp.logical_not(is_self))
        def _():
            copy.start()

        @pl.when(is_self)
        def _():
            local_bias.start()

        bias_copies.append((is_self, copy))

    home = pl.ds(pl.multiple_of(me_c * width, width), width)
    norm_copies = []
    locals_ = []
    for q in range(CHUNKS):
        part = pl.ds(q * chunk, chunk)
        local = pltpu.make_async_copy(own_ref.at[part], rows_buf.at[part, home, :], local_sem.at[q])
        local.start()
        locals_.append(local)
        for p in range(1, col_count):
            copy = pltpu.make_async_remote_copy(
                src_ref=own_ref.at[part],
                dst_ref=rows_buf.at[part, home, :],
                send_sem=norm_send.at[q, p],
                recv_sem=norm_recv.at[q],
                device_id=(me_r, lax.rem(me_c + p, col_count)),
                device_id_type=mesh_id,
            )
            copy.start()
            norm_copies.append(copy)

    direct = pieces.at[pl.ds(pl.multiple_of(parity * half, half), half)]
    pltpu.make_async_copy(direct, direct, bias_recv).wait()
    forward = pltpu.make_async_remote_copy(
        src_ref=direct,
        dst_ref=direct,
        send_sem=fwd_sem.at[0],
        recv_sem=fwd_sem.at[1],
        device_id=(sibling, me_c),
        device_id_type=mesh_id,
    )
    forward.start()

    def assemble(blocks):
        for c in range(col_count):
            for m in blocks:
                piece = pieces[(m % 2) * half + (m // 2) * col_count + c].astype(jnp.float32)
                for h in range(head_count):
                    bias_buf[h, m * depth : (m + 1) * depth, c * width : (c + 1) * width] = piece[
                        :depth, h * width : (h + 1) * width
                    ]
                if m == 0:
                    bias_buf[head_count, 0:1, c * width : (c + 1) * width] = piece[
                        depth : depth + 1, 0:width
                    ]

    even = [m for m in range(group) if m % 2 == 0]
    odd = [m for m in range(group) if m % 2 == 1]

    @pl.when(parity == 0)
    def _():
        assemble(even)

    @pl.when(parity == 1)
    def _():
        assemble(odd)

    forward.wait()

    @pl.when(parity == 0)
    def _():
        assemble(odd)

    @pl.when(parity == 1)
    def _():
        assemble(even)

    masking = 1000000000.0 * (bias_buf[head_count, 0:1, :] - 1.0)
    inner = ow_ref.shape[0]
    head_size = inner // head_count

    for q in range(CHUNKS):
        locals_[q].wait()
        arrived = pl.ds(0, (col_count - 1) * width)
        pltpu.make_async_copy(
            rows_buf.at[pl.ds(q * chunk, chunk), arrived, :],
            rows_buf.at[pl.ds(q * chunk, chunk), arrived, :],
            norm_recv.at[q],
        ).wait()

        def body(i, carry):
            updated = row_update(
                own_ref[i],
                rows_buf[i],
                bias_buf,
                masking,
                wqg_ref[...],
                wkv_ref[...],
                gb_ref[...],
                ow_ref[...],
                ob_ref[...],
                head_count,
                head_size,
            )
            out_ref[i] = updated.astype(out_ref.dtype)
            return carry

        lax.fori_loop(q * chunk, (q + 1) * chunk, body, 0)

    for copy in norm_copies:
        copy.wait_send()
    for is_self, copy in bias_copies:

        @pl.when(jnp.logical_not(is_self))
        def _():
            copy.wait_send()


def fused(pair, token_mask, norm_gain, norm_shift, bias_weight, wqg, wkv, gate_bias, out_weight, out_bias):
    own_rows, width, channels = pair.shape
    cols = lax.axis_size("cols")
    rows = lax.axis_size("rows")
    head_count = bias_weight.shape[1]
    slots = head_count + 1
    depth = own_rows
    group = rows // cols
    inner = out_weight.shape[0]
    vmem = pl.BlockSpec(memory_space=pltpu.VMEM)
    payload_shape = (own_rows + 1, head_count * width)
    return pl.pallas_call(
        functools.partial(fused_kernel, head_count),
        out_shape=jax.ShapeDtypeStruct(pair.shape, jnp.bfloat16),
        in_specs=[vmem] * 10,
        out_specs=vmem,
        scratch_shapes=[
            pltpu.VMEM(pair.shape, jnp.bfloat16),
            pltpu.VMEM(payload_shape, jnp.bfloat16),
            pltpu.VMEM((own_rows, cols * width, channels), jnp.bfloat16),
            pltpu.VMEM((rows,) + payload_shape, jnp.bfloat16),
            pltpu.VMEM((slots, group * depth, cols * width), jnp.float32),
            pltpu.SemaphoreType.DMA((CHUNKS, cols)),
            pltpu.SemaphoreType.DMA((CHUNKS,)),
            pltpu.SemaphoreType.DMA((CHUNKS,)),
            pltpu.SemaphoreType.DMA((rows // 2,)),
            pltpu.SemaphoreType.DMA(()),
            pltpu.SemaphoreType.DMA((2,)),
        ],
        compiler_params=pltpu.CompilerParams(
            has_side_effects=True, collective_id=0, vmem_limit_bytes=48 * 1024 * 1024
        ),
    )(
        pair,
        token_mask.reshape(1, width),
        norm_gain.reshape(1, channels),
        norm_shift.reshape(1, channels),
        bias_weight.T,
        wqg,
        wkv,
        gate_bias.reshape(1, inner),
        out_weight,
        out_bias.reshape(1, channels),
    )


def shards(
    pair, token_mask, norm_gain, norm_shift, in_weight, gate_bias, bias_weight, out_weight, out_bias
):
    inner = out_weight.shape[0]
    wqg = jnp.concatenate((in_weight[:, :inner], in_weight[:, 3 * inner :]), axis=1)
    wkv = in_weight[:, inner : 3 * inner]
    return fused(
        pair, token_mask, norm_gain, norm_shift, bias_weight, wqg, wkv, gate_bias, out_weight, out_bias
    )


def solution(mesh):
    placed = (P("rows", "cols", None), P("cols"), P(), P(), P(), P(), P(), P(), P())
    return jax.shard_map(
        shards, mesh=mesh, in_specs=placed, out_specs=P("rows", "cols", None), check_vma=False
    )
```

```python
import functools

import jax
import jax.numpy as jnp
from jax import lax
from jax.experimental import pallas as pl
from jax.experimental.pallas import tpu as pltpu
from jax.sharding import PartitionSpec as P


CHUNKS = 12


def row_update(own, row, bias_ref, masking, wqg, wkv, gb, ow, ob, head_count, head_size):
    inner = head_count * head_size
    qg = jnp.dot(own, wqg, preferred_element_type=jnp.float32)
    queries = (qg[:, :inner] * head_size ** (-0.5)).astype(jnp.bfloat16)
    gates = jax.nn.sigmoid(qg[:, inner:] + gb)
    keys_t = lax.dot_general(
        wkv[:, :inner], row, (((0,), (1,)), ((), ())), preferred_element_type=jnp.float32
    ).astype(jnp.bfloat16)
    values = jnp.dot(row, wkv[:, inner:], preferred_element_type=jnp.float32).astype(jnp.bfloat16)
    lane_head = lax.broadcasted_iota(jnp.int32, (1, inner), 1) // head_size
    queries_rows = own.shape[0]
    stacked = jnp.concatenate(
        [jnp.where(lane_head == h, queries, jnp.zeros_like(queries)) for h in range(head_count)],
        axis=0,
    )
    scores = jnp.dot(stacked, keys_t, preferred_element_type=jnp.float32)
    scores = scores + bias_ref[0:head_count].reshape(head_count * queries_rows, -1)
    scores = scores + masking
    top = jnp.max(scores, axis=-1, keepdims=True)
    expo = jnp.exp(scores - top)
    totals = jnp.sum(expo, axis=-1, keepdims=True)
    mixed = jnp.dot(expo.astype(jnp.bfloat16), values, preferred_element_type=jnp.float32)
    attended = jnp.zeros((queries_rows, inner), jnp.float32)
    for h in range(head_count):
        rows_h = slice(h * queries_rows, (h + 1) * queries_rows)
        attended = jnp.where(lane_head == h, mixed[rows_h] / totals[rows_h], attended)
    gated = (gates * attended).astype(jnp.bfloat16)
    return jnp.dot(gated, ow, preferred_element_type=jnp.float32) + ob


def fused_kernel(
    head_count,
    pair_ref,
    mask_ref,
    gain_ref,
    shift_ref,
    bwt_ref,
    wqg_ref,
    wkv_ref,
    gb_ref,
    ow_ref,
    ob_ref,
    out_ref,
    own_ref,
    pay_ref,
    rows_buf,
    pieces,
    bias_buf,
    norm_send,
    norm_recv,
    local_sem,
    bias_send,
    bias_recv,
    fwd_sem,
):
    col_count = lax.axis_size("cols")
    row_count = lax.axis_size("rows")
    group = row_count // col_count
    me_r = lax.axis_index("rows")
    me_c = lax.axis_index("cols")
    own_rows, width, channels = pair_ref.shape
    depth = own_rows
    chunk = own_rows // CHUNKS
    mesh_id = pl.DeviceIdType.MESH
    target_c = me_r // group
    is_home = target_c == me_c
    parity = lax.rem(me_r, 2)
    half = row_count // 2
    sibling = me_r + 1 - 2 * parity
    barrier = pltpu.get_barrier_semaphore()
    for p in range(1, col_count):
        pl.semaphore_signal(
            barrier, 1, device_id=(me_r, lax.rem(me_c + p, col_count)), device_id_type=mesh_id
        )
    pl.semaphore_signal(barrier, 1, device_id=(sibling, me_c), device_id_type=mesh_id)
    for t in range(half):
        r = 2 * t + parity

        @pl.when(jnp.logical_not(jnp.logical_and(is_home, me_r == r)))
        def _():
            pl.semaphore_signal(barrier, 1, device_id=(r, target_c), device_id_type=mesh_id)

    for u in range(group // 2):
        for c in range(col_count):
            source = group * me_c + 2 * u + parity

            @pl.when(jnp.logical_not(jnp.logical_and(source == me_r, me_c == c)))
            def _():
                pl.semaphore_signal(barrier, 1, device_id=(source, c), device_id_type=mesh_id)

    as_float = pair_ref[...].astype(jnp.float32)
    center = jnp.mean(as_float, axis=-1, keepdims=True)
    spread = jnp.mean(jnp.square(as_float - center), axis=-1, keepdims=True)
    normed = (
        (as_float - center) * lax.rsqrt(spread + 1e-05) * gain_ref[...] + shift_ref[...]
    ).astype(jnp.bfloat16)
    own_ref[...] = normed
    flat = normed.reshape(own_rows * width, channels)
    bias_t = lax.dot_general(
        bwt_ref[...], flat, (((1,), (1,)), ((), ())), preferred_element_type=jnp.float32
    ).astype(jnp.bfloat16)
    mask_row = mask_ref[...].astype(jnp.float32).astype(jnp.bfloat16)
    for h in range(head_count):
        for j in range(own_rows):
            pay_ref[j : j + 1, h * width : (h + 1) * width] = bias_t[
                h : h + 1, j * width : (j + 1) * width
            ]
        pay_ref[own_rows : own_rows + 1, h * width : (h + 1) * width] = mask_row

    pl.semaphore_wait(barrier, col_count + 2 * (half - is_home.astype(jnp.int32)))

    block = lax.rem(me_r, group)
    slot = lax.rem(block, 2) * half + (block // 2) * col_count + me_c
    local_bias = pltpu.make_async_copy(pay_ref, pieces.at[slot], bias_recv)
    bias_copies = []
    for t in range(half):
        r = 2 * t + parity
        is_self = jnp.logical_and(is_home, me_r == r)
        copy = pltpu.make_async_remote_copy(
            src_ref=pay_ref,
            dst_ref=pieces.at[slot],
            send_sem=bias_send.at[t],
            recv_sem=bias_recv,
            device_id=(r, target_c),
            device_id_type=mesh_id,
        )

        @pl.when(jnp.logical_not(is_self))
        def _():
            copy.start()

        @pl.when(is_self)
        def _():
            local_bias.start()

        bias_copies.append((is_self, copy))

    home = pl.ds(pl.multiple_of(me_c * width, width), width)
    norm_copies = []
    locals_ = []
    for q in range(CHUNKS):
        part = pl.ds(q * chunk, chunk)
        local = pltpu.make_async_copy(own_ref.at[part], rows_buf.at[part, home, :], local_sem.at[q])
        local.start()
        locals_.append(local)
        for p in list(range(1, col_count, 2)) + list(range(2, col_count, 2)):
            copy = pltpu.make_async_remote_copy(
                src_ref=own_ref.at[part],
                dst_ref=rows_buf.at[part, home, :],
                send_sem=norm_send.at[q, p],
                recv_sem=norm_recv.at[q],
                device_id=(me_r, lax.rem(me_c + p, col_count)),
                device_id_type=mesh_id,
            )
            copy.start()
            norm_copies.append(copy)

    direct = pieces.at[pl.ds(pl.multiple_of(parity * half, half), half)]
    pltpu.make_async_copy(direct, direct, bias_recv).wait()
    forward = pltpu.make_async_remote_copy(
        src_ref=direct,
        dst_ref=direct,
        send_sem=fwd_sem.at[0],
        recv_sem=fwd_sem.at[1],
        device_id=(sibling, me_c),
        device_id_type=mesh_id,
    )
    forward.start()

    def assemble(blocks):
        for c in range(col_count):
            for m in blocks:
                piece = pieces[(m % 2) * half + (m // 2) * col_count + c].astype(jnp.float32)
                for h in range(head_count):
                    bias_buf[h, m * depth : (m + 1) * depth, c * width : (c + 1) * width] = piece[
                        :depth, h * width : (h + 1) * width
                    ]
                if m == 0:
                    bias_buf[head_count, 0:1, c * width : (c + 1) * width] = piece[
                        depth : depth + 1, 0:width
                    ]

    even = [m for m in range(group) if m % 2 == 0]
    odd = [m for m in range(group) if m % 2 == 1]

    @pl.when(parity == 0)
    def _():
        assemble(even)

    @pl.when(parity == 1)
    def _():
        assemble(odd)

    forward.wait()

    @pl.when(parity == 0)
    def _():
        assemble(odd)

    @pl.when(parity == 1)
    def _():
        assemble(even)

    masking = 1000000000.0 * (bias_buf[head_count, 0:1, :] - 1.0)
    inner = ow_ref.shape[0]
    head_size = inner // head_count

    for q in range(CHUNKS):
        locals_[q].wait()
        arrived = pl.ds(0, (col_count - 1) * width)
        pltpu.make_async_copy(
            rows_buf.at[pl.ds(q * chunk, chunk), arrived, :],
            rows_buf.at[pl.ds(q * chunk, chunk), arrived, :],
            norm_recv.at[q],
        ).wait()

        def body(i, carry):
            updated = row_update(
                own_ref[i],
                rows_buf[i],
                bias_buf,
                masking,
                wqg_ref[...],
                wkv_ref[...],
                gb_ref[...],
                ow_ref[...],
                ob_ref[...],
                head_count,
                head_size,
            )
            out_ref[i] = updated.astype(out_ref.dtype)
            return carry

        lax.fori_loop(q * chunk, (q + 1) * chunk, body, 0)

    for copy in norm_copies:
        copy.wait_send()
    for is_self, copy in bias_copies:

        @pl.when(jnp.logical_not(is_self))
        def _():
            copy.wait_send()


def fused(pair, token_mask, norm_gain, norm_shift, bias_weight, wqg, wkv, gate_bias, out_weight, out_bias):
    own_rows, width, channels = pair.shape
    cols = lax.axis_size("cols")
    rows = lax.axis_size("rows")
    head_count = bias_weight.shape[1]
    slots = head_count + 1
    depth = own_rows
    group = rows // cols
    inner = out_weight.shape[0]
    vmem = pl.BlockSpec(memory_space=pltpu.VMEM)
    payload_shape = (own_rows + 1, head_count * width)
    return pl.pallas_call(
        functools.partial(fused_kernel, head_count),
        out_shape=jax.ShapeDtypeStruct(pair.shape, jnp.bfloat16),
        in_specs=[vmem] * 10,
        out_specs=vmem,
        scratch_shapes=[
            pltpu.VMEM(pair.shape, jnp.bfloat16),
            pltpu.VMEM(payload_shape, jnp.bfloat16),
            pltpu.VMEM((own_rows, cols * width, channels), jnp.bfloat16),
            pltpu.VMEM((rows,) + payload_shape, jnp.bfloat16),
            pltpu.VMEM((slots, group * depth, cols * width), jnp.float32),
            pltpu.SemaphoreType.DMA((CHUNKS, cols)),
            pltpu.SemaphoreType.DMA((CHUNKS,)),
            pltpu.SemaphoreType.DMA((CHUNKS,)),
            pltpu.SemaphoreType.DMA((rows // 2,)),
            pltpu.SemaphoreType.DMA(()),
            pltpu.SemaphoreType.DMA((2,)),
        ],
        compiler_params=pltpu.CompilerParams(
            has_side_effects=True, collective_id=0, vmem_limit_bytes=48 * 1024 * 1024
        ),
    )(
        pair,
        token_mask.reshape(1, width),
        norm_gain.reshape(1, channels),
        norm_shift.reshape(1, channels),
        bias_weight.T,
        wqg,
        wkv,
        gate_bias.reshape(1, inner),
        out_weight,
        out_bias.reshape(1, channels),
    )


def shards(
    pair, token_mask, norm_gain, norm_shift, in_weight, gate_bias, bias_weight, out_weight, out_bias
):
    inner = out_weight.shape[0]
    wqg = jnp.concatenate((in_weight[:, :inner], in_weight[:, 3 * inner :]), axis=1)
    wkv = in_weight[:, inner : 3 * inner]
    return fused(
        pair, token_mask, norm_gain, norm_shift, bias_weight, wqg, wkv, gate_bias, out_weight, out_bias
    )


def solution(mesh):
    placed = (P("rows", "cols", None), P("cols"), P(), P(), P(), P(), P(), P(), P())
    return jax.shard_map(
        shards, mesh=mesh, in_specs=placed, out_specs=P("rows", "cols", None), check_vma=False
    )
```
